32 devices in a mesh: seg: 2 (over x), ch: 16 (over z, y, core).
Axes of the slice: x: 2, y: 2, z: 4, core: 2. Of those that a mesh axis runs over, the one named last changes fastest.
Arguments:
- recording: bfloat16 [1024, 4096], P('ch', 'seg'), parts along dimension 1, may hold values from -300 to 300
- live_mask: int32 [4096], P('seg'), parts along dimension 0, may hold values 0 or 1
- window_starts: int32 [64], P('seg'), parts along dimension 0, may hold values from 0 to 512, as said below
- source_order: int32 [4], P('seg'), parts along dimension 0, may hold values from 0 to 15
Outputs:
- correlations: bfloat16 [2, 128, 4096, 128], P(None, None, ('seg', 'ch')), parts along dimension 2
The draws below stay inside these ranges and needn't reach their ends.
There are 2 independent parts, one for each index of `seg`. The reference program is written for one: setup_inputs(seed, part) draws one part's arguments, and reference() takes and returns one part's arrays. A program takes and returns all parts, laid end to end along the dimension named above; each array names one. Nothing has to cross between parts.
Inputs may be any that keep to these rules, and one draw needn't show every extreme that they name: `window_starts`: the first start is 0 and the last is 512; the others are in no order and may repeat. `source_order`: block b is the channels b * 128 to (b + 1) * 128 - 1; blocks may repeat.
All inputs are finite; a program needn't handle non-finite values.
Results may differ from the reference program's by a relative error of at most 0.0059.
Values may be sent and summed in bfloat16 or wider, within the bound.
No kernel may reach another device: no remote copies, remote signals or barrier semaphores. Data moves between devices by JAX's collectives and lax.ppermute only.
A program may use at most 128 MiB of HBM per device.

```python
import math
import jax
import jax.numpy as jnp
from jax import lax

CH_DEV = 128
WIN = 512
NF = 128
F0 = 4
LAGS = 128
HALF = 64
BAND = 64
K = 2
NWIN = 32
CHANNELS = 2048
BLOCKS = 16
TIME = 1024


def draw_recording(key, part):
    subkeys = jax.random.split(jax.random.fold_in(key, 11), 4)
    noise = jnp.clip(jax.random.normal(subkeys[0], (TIME, CHANNELS), jnp.float32), -5.0, 5.0)
    spread = math.log(10.0)
    scales = jnp.exp(jax.random.uniform(subkeys[1], (1, CHANNELS), jnp.float32, 0.0, spread))
    colour = jax.random.uniform(subkeys[2], (1, CHANNELS), jnp.float32, 0.4, 1.6)
    coloured = noise + colour * jnp.roll(noise, 1, axis=0) + 0.5 * colour * jnp.roll(noise, 2, axis=0)
    envelope = jnp.exp(jax.random.uniform(subkeys[3], (TIME // 16, 1), jnp.float32, -1.1, 1.1))
    envelope = jnp.repeat(envelope, 16, axis=0)
    return jnp.clip(0.5 * coloured * scales * envelope, -300.0, 300.0).astype(jnp.bfloat16)


def draw_window_starts(key, part):
    latest = TIME - WIN
    picked = jax.random.randint(jax.random.fold_in(key, 23), (NWIN,), 0, latest + 1, dtype=jnp.int32)
    sorting_index = jnp.arange(NWIN, dtype=jnp.int32)
    return jnp.where(sorting_index == 0, 0, jnp.where(sorting_index == NWIN - 1, latest, picked)).astype(jnp.int32)


def with_ends(values, own_key, smallest, high):
    index_at = [jax.random.randint(jax.random.fold_in(own_key, axis), (), 0, length) for axis, length in enumerate(values.shape)]
    longest = values.shape.index(max(values.shape))
    next_to = index_at[:longest] + [(index_at[longest] + 1) % values.shape[longest]] + index_at[longest + 1:]
    return values.at[tuple(index_at)].set(smallest).at[tuple(next_to)].set(high)


def setup_inputs(seed: int = 0, part: int = 0) -> dict:
    key_of = jax.random.split(jax.random.key(seed), 5)
    own_keys = jax.random.split(jax.random.fold_in(key_of[4], part), 5)
    return {
        "recording": draw_recording(jax.random.fold_in(jax.random.fold_in(key_of[4], part), 71), part),
        "live_mask": with_ends((jax.random.randint(own_keys[1], (CHANNELS,), 0, 10) < 9).astype(jnp.int32), jax.random.fold_in(own_keys[1], 1), 0, 1),
        "window_starts": draw_window_starts(jax.random.fold_in(jax.random.fold_in(key_of[4], part), 71), part),
        "source_order": jax.random.randint(own_keys[3], (K,), 0, BLOCKS).astype(jnp.int32),
    }


STABILIZER_FLOOR = 1e-06

def window_mean(values, radius, length):
    totals = jnp.cumsum(values, axis=1)
    padded = jnp.concatenate([jnp.zeros_like(totals[:, :1]), totals], axis=1)
    positions = jnp.arange(length)
    upper_end = jnp.minimum(positions + radius + 1, length)
    lower_end = jnp.maximum(positions - radius, 0)
    window_sums = padded[:, upper_end] - padded[:, lower_end]
    return window_sums / (upper_end - lower_end).astype(jnp.float32)[None, :, None]

def forward_table():
    phases = jnp.arange(WIN)[:, None] * (F0 + jnp.arange(NF))[None, :] % WIN
    angles = phases.astype(jnp.float32) * (2.0 * math.pi / WIN)
    return jnp.stack([jnp.cos(angles), -jnp.sin(angles)], axis=1).astype(jnp.bfloat16)

def inverse_table():
    phases = (F0 + jnp.arange(NF))[:, None] * (jnp.arange(LAGS)[None, :] - LAGS // 2) % WIN
    angles = phases.astype(jnp.float32) * (2.0 * math.pi / WIN)
    return jnp.stack([jnp.cos(angles), -jnp.sin(angles)], axis=0).astype(jnp.bfloat16)

def whiten(columns, window_starts, mask_portion):
    windows = jax.vmap(lambda start_shift: lax.dynamic_slice_in_dim(columns, start_shift, WIN, 0))(window_starts)
    values = windows.astype(jnp.float32)
    centred = values - lax.optimization_barrier(jnp.mean(values, axis=1, keepdims=True))
    magnitude = jnp.abs(centred).astype(jnp.bfloat16)
    running = window_mean(magnitude.astype(jnp.float32), HALF, WIN)
    normalized = (centred / (running + STABILIZER_FLOOR)).astype(jnp.bfloat16)
    channel_spectra = jnp.einsum('wjc,jrf->wrfc', normalized.astype(jnp.float32), forward_table().astype(jnp.float32))
    amplitude = jnp.sqrt(channel_spectra[:, 0] * channel_spectra[:, 0] + channel_spectra[:, 1] * channel_spectra[:, 1])
    smoothed_spectrum = window_mean(amplitude, BAND, NF)
    channel_alive_flags = mask_portion.astype(jnp.float32)
    return (channel_spectra / (smoothed_spectrum[:, None] + STABILIZER_FLOOR) * channel_alive_flags).astype(jnp.bfloat16)

def reference(recording, live_mask, window_starts, source_order):
    blocks = jnp.transpose(recording.reshape(TIME, BLOCKS, CH_DEV), (1, 0, 2))
    masks = live_mask.reshape(BLOCKS, CH_DEV)
    whitened = lax.map(lambda pair_in: whiten(pair_in[0], window_starts, pair_in[1]), (blocks, masks))
    inverse = inverse_table().astype(jnp.float32)
    factor = math.sqrt(NWIN / NF)
    results = []
    for number in range(K):
        source = lax.dynamic_index_in_dim(whitened, source_order[number], 0, keepdims=False).astype(jnp.float32)

        def against(receiver_block):
            receiver = receiver_block.astype(jnp.float32)
            real_part = jnp.einsum('wrfs,wrfc->fsc', source, receiver)
            imag_part = jnp.einsum('wfs,wfc->fsc', source[:, 0], receiver[:, 1]) - jnp.einsum('wfs,wfc->fsc', source[:, 1], receiver[:, 0])
            cross_re = (real_part / NWIN).astype(jnp.bfloat16).astype(jnp.float32)
            cross_im = (imag_part / NWIN).astype(jnp.bfloat16).astype(jnp.float32)
            lagged = jnp.einsum('fsc,ft->sct', cross_re, inverse[0]) + jnp.einsum('fsc,ft->sct', cross_im, inverse[1])
            return (lagged * factor).astype(jnp.bfloat16)
        per_block = lax.map(against, whitened)
        results.append(jnp.transpose(per_block, (1, 0, 2, 3)).reshape(CH_DEV, CHANNELS, LAGS))
    return jnp.stack(results)
```

```python
import functools
import math

import jax
import jax.numpy as jnp
from jax import lax
from jax.experimental import pallas as pl
from jax.experimental.pallas import tpu as pltpu
from jax.sharding import PartitionSpec as P

CH_DEV = 128
WIN = 512
NF = 128
F0 = 4
LAGS = 128
HALF = 64
BAND = 64

STABILIZER_FLOOR = 1e-06
TILE = 128
SPAN = TILE + 2 * HALF
SRC_STEP = 16


def forward_rows():
    phases = (F0 + jnp.arange(NF))[:, None] * jnp.arange(WIN)[None, :] % WIN
    angles = phases.astype(jnp.float32) * (2.0 * math.pi / WIN)
    return jnp.concatenate([jnp.cos(angles), -jnp.sin(angles)], axis=0).astype(jnp.bfloat16)


def inverse_rows():
    phases = (jnp.arange(LAGS)[:, None] - LAGS // 2) * (F0 + jnp.arange(NF))[None, :] % WIN
    angles = phases.astype(jnp.float32) * (2.0 * math.pi / WIN)
    return jnp.concatenate([jnp.cos(angles), -jnp.sin(angles)], axis=1).astype(jnp.bfloat16)


def time_band():
    ahead = jnp.arange(SPAN)[None, :] - jnp.arange(TILE)[:, None]
    return ((ahead >= 0) & (ahead <= 2 * HALF)).astype(jnp.bfloat16)


def bin_band():
    apart = jnp.abs(jnp.arange(NF)[:, None] - jnp.arange(NF)[None, :])
    band = (apart <= BAND).astype(jnp.bfloat16)
    return jnp.concatenate([band, band], axis=1)


def inverse_counts(length, radius):
    at = jnp.arange(length)
    counts = jnp.minimum(at + radius + 1, length) - jnp.maximum(at - radius, 0)
    return jnp.broadcast_to((1.0 / counts.astype(jnp.float32))[:, None], (length, CH_DEV))


def pack_kernel(order_ref, x_ref, out_ref):
    blocks = out_ref.shape[0]
    numbers = order_ref.shape[0]
    for block in range(blocks):
        out_ref[block, :, :CH_DEV] = x_ref[:, block * CH_DEV : (block + 1) * CH_DEV]
        first = pl.multiple_of(order_ref[block % numbers] * CH_DEV, CH_DEV)
        out_ref[block, :, CH_DEV:] = x_ref[:, pl.ds(first, CH_DEV)]


def pack(order, recording):
    rows, channels = recording.shape
    blocks = channels // CH_DEV
    return pl.pallas_call(
        pack_kernel,
        out_shape=jax.ShapeDtypeStruct((blocks, rows, 2 * CH_DEV), recording.dtype),
        in_specs=[pl.BlockSpec(memory_space=pltpu.SMEM), pl.BlockSpec(memory_space=pltpu.VMEM)],
        out_specs=pl.BlockSpec(memory_space=pltpu.VMEM),
        name="pack",
    )(order, recording)


def whiten_kernel(
    starts_ref, block_ref, x_ref, mask_ref, forward_ref, band_ref, bins_ref, tcount_ref, fcount_ref,
    out_ref, xf, cen, mag, nrm, spec,
):
    windows = starts_ref.shape[0]
    xf[...] = x_ref[...].astype(jnp.float32)
    first = pl.multiple_of(block_ref[0] * CH_DEV, CH_DEV)
    mask = mask_ref[:, pl.ds(first, CH_DEV)].astype(jnp.float32)
    mask = jnp.concatenate([mask, mask], axis=1)
    edge = jnp.zeros((HALF, 2 * CH_DEV), jnp.bfloat16)
    mag[:HALF, :] = edge
    mag[HALF + WIN :, :] = edge

    def pair(number, carry):
        for side in range(2):
            lanes = slice(side * CH_DEV, (side + 1) * CH_DEV)
            start = starts_ref[2 * number + side]
            values = xf[pl.ds(start, WIN), :]
            mean = jnp.sum(values, axis=0, keepdims=True) * (1.0 / WIN)
            centred = values - mean
            cen[:, lanes] = centred
            mag[HALF : HALF + WIN, lanes] = jnp.abs(centred).astype(jnp.bfloat16)
        for tile in range(WIN // TILE):
            rows = slice(tile * TILE, (tile + 1) * TILE)
            sums = jnp.dot(
                band_ref[...], mag[tile * TILE : tile * TILE + SPAN, :], preferred_element_type=jnp.float32
            )
            count = tcount_ref[rows, :]
            running = sums * jnp.concatenate([count, count], axis=1)
            nrm[rows, :] = (cen[rows, :] / (running + STABILIZER_FLOOR)).astype(jnp.bfloat16)
        spectra = jnp.dot(forward_ref[...], nrm[...], preferred_element_type=jnp.float32)
        re, im = spectra[:NF, :], spectra[NF:, :]
        amplitude = jnp.sqrt(re * re + im * im)
        high = amplitude.astype(jnp.bfloat16)
        low = (amplitude - high.astype(jnp.float32)).astype(jnp.bfloat16)
        sums = jnp.dot(
            bins_ref[...], jnp.concatenate([high, low], axis=0), preferred_element_type=jnp.float32
        )
        count = fcount_ref[...]
        smooth = sums * jnp.concatenate([count, count], axis=1)
        scale = mask / (smooth + STABILIZER_FLOOR)
        for part, values in enumerate((re * scale, im * scale)):
            for side in range(2):
                row = part * windows + 2 * number + side
                spec[pl.ds(row, NF, stride=2 * windows), :] = values[:, side * CH_DEV : (side + 1) * CH_DEV]
        return carry

    lax.fori_loop(0, windows // 2, pair, 0)

    def emit(f, carry):
        rows = pl.ds(pl.multiple_of(f * 2 * windows, 2 * windows), 2 * windows)
        out_ref[f] = spec[rows, :].astype(jnp.bfloat16)
        return carry

    lax.fori_loop(0, NF, emit, 0, unroll=8)


def whiten(samples, column, starts, block, live_mask, tables):
    length = samples.shape[0]
    windows = starts.shape[0]
    channels = live_mask.shape[0]
    smem = pl.BlockSpec(memory_space=pltpu.SMEM)
    whole = lambda a: pl.BlockSpec(a.shape, lambda i: (0,) * a.ndim)
    return pl.pallas_call(
        whiten_kernel,
        grid=(1,),
        out_shape=jax.ShapeDtypeStruct((NF, 2 * windows, CH_DEV), jnp.bfloat16),
        in_specs=[
            smem,
            smem,
            pl.BlockSpec((length, CH_DEV), lambda i: (0, column)),
            pl.BlockSpec((1, channels), lambda i: (0, 0)),
        ]
        + [whole(t) for t in tables],
        out_specs=pl.BlockSpec((NF, 2 * windows, CH_DEV), lambda i: (0, 0, 0)),
        scratch_shapes=[
            pltpu.VMEM((length, CH_DEV), jnp.float32),
            pltpu.VMEM((WIN, 2 * CH_DEV), jnp.float32),
            pltpu.VMEM((WIN + 2 * HALF, 2 * CH_DEV), jnp.bfloat16),
            pltpu.VMEM((WIN, 2 * CH_DEV), jnp.bfloat16),
            pltpu.VMEM((NF * 2 * windows, CH_DEV), jnp.float32),
        ],
        cost_estimate=pl.CostEstimate(flops=6_000_000_000, bytes_accessed=3_000_000, transcendentals=0),
        name="whiten",
    )(starts, block, samples, live_mask.reshape(1, channels), *tables)


def correlate_kernel(parity_ref, here_ref, there_ref, own_ref, inverse_ref, out_ref, cross_re, cross_im):
    rows = own_ref.shape[1]
    half = rows // 2
    scale = math.sqrt(half / NF) / half

    @pl.when((pl.program_id(0) == 0) & (pl.program_id(1) == 0))
    def _():
        def bin_step(f, carry):
            source = jnp.concatenate([here_ref[f], there_ref[f]], axis=1)
            own = own_ref[f]
            swapped = jnp.concatenate([own[half:], -own[:half]], axis=0)
            product = lax.dot_general(
                source,
                jnp.concatenate([own, swapped], axis=1),
                (((0,), (0,)), ((), ())),
                preferred_element_type=jnp.float32,
            )
            at = pl.ds(f, 2 * CH_DEV, stride=NF)
            cross_re[at, :] = product[:, :CH_DEV]
            cross_im[at, :] = product[:, CH_DEV:]
            return carry

        lax.fori_loop(0, NF, bin_step, 0, unroll=2)

    base = (pl.program_id(0) * CH_DEV + pl.program_id(1) * SRC_STEP) * NF
    for s in range(0, SRC_STEP, 2):
        columns = []
        for one in (s, s + 1):
            at = pl.ds(pl.multiple_of(base + one * NF, NF), NF)
            columns.append(
                jnp.concatenate(
                    [cross_re[at, :].astype(jnp.bfloat16), cross_im[at, :].astype(jnp.bfloat16)], axis=0
                )
            )
        lagged = jnp.dot(
            inverse_ref[...], jnp.concatenate(columns, axis=1), preferred_element_type=jnp.float32
        )
        lagged = (lagged * scale).astype(jnp.bfloat16)
        for side in range(2):
            out_ref[0, s + side] = lagged[:, side * CH_DEV : (side + 1) * CH_DEV].T


def correlate(parity, here, there, own, inverse):
    spectrum = pl.BlockSpec(here.shape, lambda k, s, p: (0, 0, 0), pipeline_mode=pl.Buffered(1))
    return pl.pallas_call(
        correlate_kernel,
        grid_spec=pltpu.PrefetchScalarGridSpec(
            num_scalar_prefetch=1,
            grid=(2, CH_DEV // SRC_STEP),
            in_specs=[spectrum, spectrum, spectrum, pl.BlockSpec(inverse.shape, lambda k, s, p: (0, 0))],
            out_specs=pl.BlockSpec(
                (1, SRC_STEP, CH_DEV, LAGS), lambda k, s, p: ((k + p[0]) % 2, s, 0, 0)
            ),
            scratch_shapes=[pltpu.VMEM((2 * CH_DEV * NF, CH_DEV), jnp.float32)] * 2,
        ),
        out_shape=jax.ShapeDtypeStruct((2, CH_DEV, CH_DEV, LAGS), jnp.bfloat16),
        name="correlate",
        compiler_params=pltpu.CompilerParams(vmem_limit_bytes=60_000 * 1024),
    )(parity, here, there, own, inverse)


def local(recording, live_mask, window_starts, source_order):
    position = lax.axis_index("ch").astype(jnp.int32)
    parity = position % 2
    sent = pack(source_order, recording)
    arrived = lax.all_to_all(sent, "ch", split_axis=0, concat_axis=0, tiled=True)
    samples = arrived.reshape(-1, 2 * CH_DEV)
    tables = (
        forward_rows(),
        time_band(),
        bin_band(),
        inverse_counts(WIN, HALF),
        inverse_counts(NF, BAND),
    )
    own_source = lax.dynamic_slice_in_dim(source_order, parity, 1, 0)
    here = whiten(samples, 1, window_starts, own_source, live_mask, tables)
    devices = lax.axis_size("ch")
    there = lax.ppermute(here, "ch", [(i, i ^ 1) for i in range(devices)])
    own = whiten(samples, 0, window_starts, position[None], live_mask, tables)
    return correlate(parity[None], here, there, own, inverse_rows())


def solution(mesh):
    in_specs = (P("ch", "seg"), P("seg"), P("seg"), P("seg"))
    out_specs = P(None, None, ("seg", "ch"), None)
    return jax.shard_map(local, mesh=mesh, in_specs=in_specs, out_specs=out_specs, check_vma=False)
```

```python
import functools
import math

import jax
import jax.numpy as jnp
from jax import lax
from jax.experimental import pallas as pl
from jax.experimental.pallas import tpu as pltpu
from jax.sharding import PartitionSpec as P

CH_DEV = 128
WIN = 512
NF = 128
F0 = 4
LAGS = 128
HALF = 64
BAND = 64

STABILIZER_FLOOR = 1e-06
TILE = 128
SPAN = TILE + 2 * HALF
SRC_STEP = 32
BIN_STEP = 32
PITCH = NF + 1


def forward_rows():
    phases = (F0 + jnp.arange(NF))[:, None] * jnp.arange(WIN)[None, :] % WIN
    angles = phases.astype(jnp.float32) * (2.0 * math.pi / WIN)
    return jnp.concatenate([jnp.cos(angles), -jnp.sin(angles)], axis=0).astype(jnp.bfloat16)


def inverse_rows():
    phases = (jnp.arange(LAGS)[:, None] - LAGS // 2) * (F0 + jnp.arange(NF))[None, :] % WIN
    angles = phases.astype(jnp.float32) * (2.0 * math.pi / WIN)
    return jnp.concatenate([jnp.cos(angles), -jnp.sin(angles)], axis=1).astype(jnp.bfloat16)


def time_band():
    ahead = jnp.arange(SPAN)[None, :] - jnp.arange(TILE)[:, None]
    return ((ahead >= 0) & (ahead <= 2 * HALF)).astype(jnp.bfloat16)


def bin_band():
    apart = jnp.abs(jnp.arange(NF)[:, None] - jnp.arange(NF)[None, :])
    band = (apart <= BAND).astype(jnp.bfloat16)
    return jnp.concatenate([band, band], axis=1)


def inverse_counts(length, radius):
    at = jnp.arange(length)
    counts = jnp.minimum(at + radius + 1, length) - jnp.maximum(at - radius, 0)
    return jnp.broadcast_to((1.0 / counts.astype(jnp.float32))[:, None], (length, CH_DEV))


def pack_kernel(order_ref, x_ref, out_ref):
    blocks = out_ref.shape[0]
    numbers = order_ref.shape[0]
    for block in range(blocks):
        out_ref[block, :, :CH_DEV] = x_ref[:, block * CH_DEV : (block + 1) * CH_DEV]
        first = pl.multiple_of(order_ref[block % numbers] * CH_DEV, CH_DEV)
        out_ref[block, :, CH_DEV:] = x_ref[:, pl.ds(first, CH_DEV)]


def pack(order, recording):
    rows, channels = recording.shape
    blocks = channels // CH_DEV
    return pl.pallas_call(
        pack_kernel,
        out_shape=jax.ShapeDtypeStruct((blocks, rows, 2 * CH_DEV), recording.dtype),
        in_specs=[pl.BlockSpec(memory_space=pltpu.SMEM), pl.BlockSpec(memory_space=pltpu.VMEM)],
        out_specs=pl.BlockSpec(memory_space=pltpu.VMEM),
        name="pack",
    )(order, recording)


def whiten_kernel(
    starts_ref, block_ref, x_ref, first_ref, mask_ref, forward_ref, band_ref, bins_ref, tcount_ref, fcount_ref,
    out_ref, xf, means, cen, mag, nrm, spec,
):
    length = x_ref.shape[0]
    windows = starts_ref.shape[0]
    pairs = windows // 2
    pitch = 2 * windows + 1
    xf[...] = x_ref[...].astype(jnp.float32)
    at = lax.broadcasted_iota(jnp.int32, (windows, length), 1) - first_ref[...]
    inside = ((at >= 0) & (at < WIN)).astype(jnp.bfloat16)
    means[...] = jnp.dot(inside, x_ref[...], preferred_element_type=jnp.float32) * (1.0 / WIN)
    first = pl.multiple_of(block_ref[0] * CH_DEV, CH_DEV)
    mask = mask_ref[:, pl.ds(first, CH_DEV)].astype(jnp.float32)
    mask = jnp.concatenate([mask, mask], axis=1)
    edge = jnp.zeros((HALF, 2 * CH_DEV), jnp.bfloat16)
    mag[:HALF, :] = edge
    mag[HALF + WIN :, :] = edge
    interior = 1.0 / (2 * HALF + 1)

    def transform(pair):
        spectra = jnp.dot(forward_ref[...], nrm[...], preferred_element_type=jnp.float32)
        re, im = spectra[:NF, :], spectra[NF:, :]
        power = re * re + im * im
        amplitude = power * lax.rsqrt(jnp.maximum(power, 1e-37))
        high = amplitude.astype(jnp.bfloat16)
        low = (amplitude - high.astype(jnp.float32)).astype(jnp.bfloat16)
        sums = jnp.dot(
            bins_ref[...], jnp.concatenate([high, low], axis=0), preferred_element_type=jnp.float32
        )
        count = fcount_ref[...]
        smooth = sums * jnp.concatenate([count, count], axis=1)
        scale = mask / (smooth + STABILIZER_FLOOR)
        for part, values in enumerate((re * scale, im * scale)):
            for side in range(2):
                row = part * windows + 2 * pair + side
                spec[pl.ds(row, NF, stride=pitch), :] = values[:, side * CH_DEV : (side + 1) * CH_DEV]

    def normalize(pair):
        for side in range(2):
            lanes = slice(side * CH_DEV, (side + 1) * CH_DEV)
            window = 2 * pair + side
            centred = xf[pl.ds(starts_ref[window], WIN), :] - means[pl.ds(window, 1), :]
            cen[:, lanes] = centred
            mag[HALF : HALF + WIN, lanes] = jnp.abs(centred.astype(jnp.bfloat16))
        for tile in range(WIN // TILE):
            rows = slice(tile * TILE, (tile + 1) * TILE)
            sums = jnp.dot(
                band_ref[...], mag[tile * TILE : tile * TILE + SPAN, :], preferred_element_type=jnp.float32
            )
            if HALF <= tile * TILE and (tile + 1) * TILE <= WIN - HALF:
                running = sums * interior
            else:
                count = tcount_ref[rows, :]
                running = sums * jnp.concatenate([count, count], axis=1)
            nrm[rows, :] = (cen[rows, :] / (running + STABILIZER_FLOOR)).astype(jnp.bfloat16)

    def step(number, carry):
        transform(jnp.maximum(number - 1, 0))
        normalize(jnp.minimum(number, pairs - 1))
        return carry

    lax.fori_loop(0, pairs + 1, step, 0)

    def emit(f, carry):
        out_ref[f] = spec[pl.ds(f * pitch, 2 * windows), :].astype(jnp.bfloat16)
        return carry

    lax.fori_loop(0, NF, emit, 0, unroll=8)


def whiten(samples, column, starts, block, live_mask, tables):
    length = samples.shape[0]
    windows = starts.shape[0]
    channels = live_mask.shape[0]
    smem = pl.BlockSpec(memory_space=pltpu.SMEM)
    whole = lambda a: pl.BlockSpec(a.shape, lambda i: (0,) * a.ndim)
    return pl.pallas_call(
        whiten_kernel,
        grid=(1,),
        out_shape=jax.ShapeDtypeStruct((NF, 2 * windows, CH_DEV), jnp.bfloat16),
        in_specs=[
            smem,
            smem,
            pl.BlockSpec((length, CH_DEV), lambda i: (0, column)),
            pl.BlockSpec((windows, 1), lambda i: (0, 0)),
            pl.BlockSpec((1, channels), lambda i: (0, 0)),
        ]
        + [whole(t) for t in tables],
        out_specs=pl.BlockSpec((NF, 2 * windows, CH_DEV), lambda i: (0, 0, 0)),
        scratch_shapes=[
            pltpu.VMEM((length, CH_DEV), jnp.float32),
            pltpu.VMEM((windows, CH_DEV), jnp.float32),
            pltpu.VMEM((WIN, 2 * CH_DEV), jnp.float32),
            pltpu.VMEM((WIN + 2 * HALF, 2 * CH_DEV), jnp.bfloat16),
            pltpu.VMEM((WIN, 2 * CH_DEV), jnp.bfloat16),
            pltpu.VMEM((NF * (2 * windows + 1), CH_DEV), jnp.float32),
        ],
        cost_estimate=pl.CostEstimate(flops=6_000_000_000, bytes_accessed=3_000_000, transcendentals=0),
        name="whiten",
        compiler_params=pltpu.CompilerParams(vmem_limit_bytes=14 * 1024 * 1024),
    )(starts, block, samples, starts.reshape(windows, 1), live_mask.reshape(1, channels), *tables)


def correlate_kernel(parity_ref, here_ref, there_ref, own_ref, inverse_ref, out_ref, cross_re, cross_im, lag):
    bins, rows = own_ref.shape[0], own_ref.shape[1]
    half = rows // 2
    scale = math.sqrt(half / NF) / half
    step = pl.program_id(0)
    crossing = NF // bins

    @pl.when(step < crossing)
    def _():
        for f in range(bins):
            source = jnp.concatenate([here_ref[f], there_ref[f]], axis=1)
            own = own_ref[f]
            swapped = jnp.concatenate([own[half:], -own[:half]], axis=0)
            product = lax.dot_general(
                source,
                jnp.concatenate([own, swapped], axis=1),
                (((0,), (0,)), ((), ())),
                preferred_element_type=jnp.float32,
            )
            at = pl.ds(step * bins + f, 2 * CH_DEV, stride=PITCH)
            cross_re[at, :] = product[:, :CH_DEV]
            cross_im[at, :] = product[:, CH_DEV:]

    @pl.when(step >= crossing)
    def _():
        for s in range(SRC_STEP):
            out_ref[0, s] = lag[s].T
        chunk = jnp.minimum(step - crossing, 2 * CH_DEV // SRC_STEP - 1)
        base = chunk * SRC_STEP * PITCH
        for s in range(0, SRC_STEP, 2):
            columns = []
            for one in (s, s + 1):
                at = pl.ds(base + one * PITCH, NF)
                columns.append(
                    jnp.concatenate(
                        [cross_re[at, :].astype(jnp.bfloat16), cross_im[at, :].astype(jnp.bfloat16)], axis=0
                    )
                )
            lagged = jnp.dot(
                inverse_ref[...], jnp.concatenate(columns, axis=1), preferred_element_type=jnp.float32
            )
            lagged = (lagged * scale).astype(jnp.bfloat16)
            for side in range(2):
                lag[s + side] = lagged[:, side * CH_DEV : (side + 1) * CH_DEV]


def correlate(parity, here, there, own, inverse):
    crossing = NF // BIN_STEP
    chunks = CH_DEV // SRC_STEP
    spectrum = pl.BlockSpec((BIN_STEP,) + here.shape[1:], lambda i, p: (jnp.minimum(i, crossing - 1), 0, 0))

    def placed(i, p):
        chunk = jnp.clip(i - crossing - 1, 0, 2 * chunks - 1)
        return (chunk // chunks + p[0]) % 2, chunk % chunks, 0, 0

    return pl.pallas_call(
        correlate_kernel,
        grid_spec=pltpu.PrefetchScalarGridSpec(
            num_scalar_prefetch=1,
            grid=(crossing + 2 * chunks + 1,),
            in_specs=[spectrum, spectrum, spectrum, pl.BlockSpec(inverse.shape, lambda i, p: (0, 0))],
            out_specs=pl.BlockSpec((1, SRC_STEP, CH_DEV, LAGS), placed),
            scratch_shapes=[pltpu.VMEM((2 * CH_DEV * PITCH, CH_DEV), jnp.float32)] * 2
            + [pltpu.VMEM((SRC_STEP, LAGS, CH_DEV), jnp.bfloat16)],
        ),
        out_shape=jax.ShapeDtypeStruct((2, CH_DEV, CH_DEV, LAGS), jnp.bfloat16),
        name="correlate",
        compiler_params=pltpu.CompilerParams(vmem_limit_bytes=48 * 1024 * 1024),
    )(parity, here, there, own, inverse)


def local(recording, live_mask, window_starts, source_order):
    position = lax.axis_index("ch").astype(jnp.int32)
    parity = position % 2
    sent = pack(source_order, recording)
    arrived = lax.all_to_all(sent, "ch", split_axis=0, concat_axis=0, tiled=True)
    samples = arrived.reshape(-1, 2 * CH_DEV)
    tables = (
        forward_rows(),
        time_band(),
        bin_band(),
        inverse_counts(WIN, HALF),
        inverse_counts(NF, BAND),
    )
    own_source = lax.dynamic_slice_in_dim(source_order, parity, 1, 0)
    here = whiten(samples, 1, window_starts, own_source, live_mask, tables)
    devices = lax.axis_size("ch")
    there = lax.ppermute(here, "ch", [(i, i ^ 1) for i in range(devices)])
    own = whiten(samples, 0, window_starts, position[None], live_mask, tables)
    return correlate(parity[None], here, there, own, inverse_rows())


def solution(mesh):
    in_specs = (P("ch", "seg"), P("seg"), P("seg"), P("seg"))
    out_specs = P(None, None, ("seg", "ch"), None)
    return jax.shard_map(local, mesh=mesh, in_specs=in_specs, out_specs=out_specs, check_vma=False)
```

```python
import functools
import math

import jax
import jax.numpy as jnp
from jax import lax
from jax.experimental import pallas as pl
from jax.experimental.pallas import tpu as pltpu
from jax.sharding import PartitionSpec as P

CH_DEV = 128
WIN = 512
NF = 128
F0 = 4
LAGS = 128
HALF = 64
BAND = 64

STABILIZER_FLOOR = 1e-06
TILE = 128
SPAN = TILE + 2 * HALF
SRC_STEP = 32
BIN_STEP = 32
PITCH = NF + 1


def forward_rows():
    phases = (F0 + jnp.arange(NF))[:, None] * jnp.arange(WIN)[None, :] % WIN
    angles = phases.astype(jnp.float32) * (2.0 * math.pi / WIN)
    return jnp.concatenate([jnp.cos(angles), -jnp.sin(angles)], axis=0).astype(jnp.bfloat16)


def inverse_rows():
    phases = (jnp.arange(LAGS)[:, None] - LAGS // 2) * (F0 + jnp.arange(NF))[None, :] % WIN
    angles = phases.astype(jnp.float32) * (2.0 * math.pi / WIN)
    return jnp.concatenate([jnp.cos(angles), -jnp.sin(angles)], axis=1).astype(jnp.bfloat16)


def time_band():
    ahead = jnp.arange(SPAN)[None, :] - jnp.arange(TILE)[:, None]
    return ((ahead >= 0) & (ahead <= 2 * HALF)).astype(jnp.bfloat16)


def bin_band():
    apart = jnp.abs(jnp.arange(NF)[:, None] - jnp.arange(NF)[None, :])
    band = (apart <= BAND).astype(jnp.bfloat16)
    return jnp.concatenate([band, band], axis=1)


def inverse_counts(length, radius):
    at = jnp.arange(length)
    counts = jnp.minimum(at + radius + 1, length) - jnp.maximum(at - radius, 0)
    return jnp.broadcast_to((1.0 / counts.astype(jnp.float32))[:, None], (length, CH_DEV))


def pack_kernel(order_ref, x_ref, out_ref):
    blocks = out_ref.shape[0]
    numbers = order_ref.shape[0]
    for block in range(blocks):
        out_ref[block, :, :CH_DEV] = x_ref[:, block * CH_DEV : (block + 1) * CH_DEV]
        first = pl.multiple_of(order_ref[block % numbers] * CH_DEV, CH_DEV)
        out_ref[block, :, CH_DEV:] = x_ref[:, pl.ds(first, CH_DEV)]


def pack(order, recording):
    rows, channels = recording.shape
    blocks = channels // CH_DEV
    return pl.pallas_call(
        pack_kernel,
        out_shape=jax.ShapeDtypeStruct((blocks, rows, 2 * CH_DEV), recording.dtype),
        in_specs=[pl.BlockSpec(memory_space=pltpu.SMEM), pl.BlockSpec(memory_space=pltpu.VMEM)],
        out_specs=pl.BlockSpec(memory_space=pltpu.VMEM),
        name="pack",
    )(order, recording)


def whiten_kernel(
    starts_ref, block_ref, x_ref, first_ref, mask_ref, forward_ref, band_ref, bins_ref, tcount_ref, fcount_ref,
    out_ref, xf, means, cen, mag, nrm, total, spc, spec,
):
    length = x_ref.shape[0]
    windows = starts_ref.shape[0]
    pairs = windows // 2
    pitch = 2 * windows + 1
    xf[...] = x_ref[...].astype(jnp.float32)
    at = lax.broadcasted_iota(jnp.int32, (windows, length), 1) - first_ref[...]
    inside = ((at >= 0) & (at < WIN)).astype(jnp.bfloat16)
    means[...] = jnp.dot(inside, x_ref[...], preferred_element_type=jnp.float32) * (1.0 / WIN)
    first = pl.multiple_of(block_ref[0] * CH_DEV, CH_DEV)
    mask = mask_ref[:, pl.ds(first, CH_DEV)].astype(jnp.float32)
    mask = jnp.concatenate([mask, mask], axis=1)
    edge = jnp.zeros((HALF, CH_DEV), jnp.bfloat16)
    for slot in range(2):
        for side in range(2):
            mag[slot][side][:HALF, :] = edge
            mag[slot][side][HALF + WIN :, :] = edge
    interior = 1.0 / (2 * HALF + 1)

    def center(pair, slot):
        for side in range(2):
            window = 2 * pair + side
            centred = xf[pl.ds(starts_ref[window], WIN), :] - means[pl.ds(window, 1), :]
            cen[slot][side][...] = centred
            mag[slot][side][HALF : HALF + WIN, :] = jnp.abs(centred).astype(jnp.bfloat16)

    def band(slot):
        for tile in range(WIN // TILE):
            rows = slice(tile * TILE, tile * TILE + SPAN)
            total[slot][tile * TILE : (tile + 1) * TILE, :] = jnp.dot(
                band_ref[...],
                jnp.concatenate([mag[slot][0][rows, :], mag[slot][1][rows, :]], axis=1),
                preferred_element_type=jnp.float32,
            )

    def normalize(pair, slot):
        for tile in range(WIN // TILE):
            rows = slice(tile * TILE, (tile + 1) * TILE)
            for side in range(2):
                running = total[slot][rows, side * CH_DEV : (side + 1) * CH_DEV]
                if HALF <= tile * TILE and (tile + 1) * TILE <= WIN - HALF:
                    running = running * interior
                else:
                    running = running * tcount_ref[rows, :]
                nrm[slot][side][rows, :] = (cen[slot][side][rows, :] / (running + STABILIZER_FLOOR)).astype(
                    jnp.bfloat16
                )

    def transform(slot):
        spc[slot][...] = jnp.dot(
            forward_ref[...],
            jnp.concatenate([nrm[slot][0][...], nrm[slot][1][...]], axis=1),
            preferred_element_type=jnp.float32,
        )

    def spectral(pair, slot):
        re, im = spc[slot][:NF, :], spc[slot][NF:, :]
        power = re * re + im * im
        amplitude = power * lax.rsqrt(jnp.maximum(power, 1e-37))
        high = amplitude.astype(jnp.bfloat16)
        low = (amplitude - high.astype(jnp.float32)).astype(jnp.bfloat16)
        sums = jnp.dot(
            bins_ref[...], jnp.concatenate([high, low], axis=0), preferred_element_type=jnp.float32
        )
        count = fcount_ref[...]
        smooth = sums * jnp.concatenate([count, count], axis=1)
        scale = mask / (smooth + STABILIZER_FLOOR)
        for part in range(2):
            values = spc[slot][part * NF : (part + 1) * NF, :] * scale
            for side in range(2):
                row = part * windows + 2 * pair + side
                spec[pl.ds(row, NF, stride=pitch), :] = values[:, side * CH_DEV : (side + 1) * CH_DEV]

    def step(index, carry):
        for phase in range(6):
            number, now, before = 6 * index + phase, phase % 2, (phase + 1) % 2
            normalize(jnp.clip(number - 1, 0, pairs - 1), before)
            transform(before)
            center(jnp.minimum(number, pairs - 1), now)
            band(now)
            spectral(jnp.maximum(number - 2, 0), now)
        return carry

    lax.fori_loop(0, (pairs + 2 + 6 - 1) // 6, step, 0)

    def emit(f, carry):
        out_ref[f] = spec[pl.ds(f * pitch, 2 * windows), :].astype(jnp.bfloat16)
        return carry

    lax.fori_loop(0, NF, emit, 0, unroll=8)


def whiten(samples, column, starts, block, live_mask, tables):
    length = samples.shape[0]
    windows = starts.shape[0]
    channels = live_mask.shape[0]
    smem = pl.BlockSpec(memory_space=pltpu.SMEM)
    whole = lambda a: pl.BlockSpec(a.shape, lambda i: (0,) * a.ndim)
    return pl.pallas_call(
        whiten_kernel,
        grid=(1,),
        out_shape=jax.ShapeDtypeStruct((NF, 2 * windows, CH_DEV), jnp.bfloat16),
        in_specs=[
            smem,
            smem,
            pl.BlockSpec((length, CH_DEV), lambda i: (0, column)),
            pl.BlockSpec((windows, 1), lambda i: (0, 0)),
            pl.BlockSpec((1, channels), lambda i: (0, 0)),
        ]
        + [whole(t) for t in tables],
        out_specs=pl.BlockSpec((NF, 2 * windows, CH_DEV), lambda i: (0, 0, 0)),
        scratch_shapes=[
            pltpu.VMEM((length, CH_DEV), jnp.float32),
            pltpu.VMEM((windows, CH_DEV), jnp.float32),
            [[pltpu.VMEM((WIN, CH_DEV), jnp.float32)] * 2] * 2,
            [[pltpu.VMEM((WIN + 2 * HALF, CH_DEV), jnp.bfloat16)] * 2] * 2,
            [[pltpu.VMEM((WIN, CH_DEV), jnp.bfloat16)] * 2] * 2,
            [pltpu.VMEM((WIN, 2 * CH_DEV), jnp.float32)] * 2,
            [pltpu.VMEM((2 * NF, 2 * CH_DEV), jnp.float32)] * 2,
            pltpu.VMEM((NF * (2 * windows + 1), CH_DEV), jnp.float32),
        ],
        cost_estimate=pl.CostEstimate(flops=6_000_000_000, bytes_accessed=3_000_000, transcendentals=0),
        name="whiten",
        compiler_params=pltpu.CompilerParams(vmem_limit_bytes=14 * 1024 * 1024),
    )(starts, block, samples, starts.reshape(windows, 1), live_mask.reshape(1, channels), *tables)


def correlate_kernel(parity_ref, here_ref, there_ref, own_ref, inverse_ref, out_ref, cross_re, cross_im, lag):
    bins, rows = own_ref.shape[0], own_ref.shape[1]
    half = rows // 2
    scale = math.sqrt(half / NF) / half
    step = pl.program_id(0)
    crossing = NF // bins

    @pl.when(step < crossing)
    def _():
        for f in range(bins):
            source = jnp.concatenate([here_ref[f], there_ref[f]], axis=1)
            own = own_ref[f]
            swapped = jnp.concatenate([own[half:], -own[:half]], axis=0)
            product = lax.dot_general(
                source,
                jnp.concatenate([own, swapped], axis=1),
                (((0,), (0,)), ((), ())),
                preferred_element_type=jnp.float32,
            )
            at = pl.ds(step * bins + f, 2 * CH_DEV, stride=PITCH)
            cross_re[at, :] = product[:, :CH_DEV]
            cross_im[at, :] = product[:, CH_DEV:]

    @pl.when(step >= crossing)
    def _():
        for s in range(SRC_STEP):
            out_ref[0, s] = lag[s].T
        chunk = jnp.minimum(step - crossing, 2 * CH_DEV // SRC_STEP - 1)
        base = chunk * SRC_STEP * PITCH
        for s in range(0, SRC_STEP, 2):
            columns = []
            for one in (s, s + 1):
                at = pl.ds(base + one * PITCH, NF)
                columns.append(
                    jnp.concatenate(
                        [cross_re[at, :].astype(jnp.bfloat16), cross_im[at, :].astype(jnp.bfloat16)], axis=0
                    )
                )
            lagged = jnp.dot(
                inverse_ref[...], jnp.concatenate(columns, axis=1), preferred_element_type=jnp.float32
            )
            lagged = (lagged * scale).astype(jnp.bfloat16)
            for side in range(2):
                lag[s + side] = lagged[:, side * CH_DEV : (side + 1) * CH_DEV]


def correlate(parity, here, there, own, inverse):
    crossing = NF // BIN_STEP
    chunks = CH_DEV // SRC_STEP
    spectrum = pl.BlockSpec((BIN_STEP,) + here.shape[1:], lambda i, p: (jnp.minimum(i, crossing - 1), 0, 0))

    def placed(i, p):
        chunk = jnp.clip(i - crossing - 1, 0, 2 * chunks - 1)
        return (chunk // chunks + p[0]) % 2, chunk % chunks, 0, 0

    return pl.pallas_call(
        correlate_kernel,
        grid_spec=pltpu.PrefetchScalarGridSpec(
            num_scalar_prefetch=1,
            grid=(crossing + 2 * chunks + 1,),
            in_specs=[spectrum, spectrum, spectrum, pl.BlockSpec(inverse.shape, lambda i, p: (0, 0))],
            out_specs=pl.BlockSpec((1, SRC_STEP, CH_DEV, LAGS), placed),
            scratch_shapes=[pltpu.VMEM((2 * CH_DEV * PITCH, CH_DEV), jnp.float32)] * 2
            + [pltpu.VMEM((SRC_STEP, LAGS, CH_DEV), jnp.bfloat16)],
        ),
        out_shape=jax.ShapeDtypeStruct((2, CH_DEV, CH_DEV, LAGS), jnp.bfloat16),
        name="correlate",
        compiler_params=pltpu.CompilerParams(vmem_limit_bytes=40 * 1024 * 1024),
    )(parity, here, there, own, inverse)


def local(recording, live_mask, window_starts, source_order):
    position = lax.axis_index("ch").astype(jnp.int32)
    parity = position % 2
    sent = pack(source_order, recording)
    arrived = lax.all_to_all(sent, "ch", split_axis=0, concat_axis=0, tiled=True)
    samples = arrived.reshape(-1, 2 * CH_DEV)
    tables = (
        forward_rows(),
        time_band(),
        bin_band(),
        inverse_counts(WIN, HALF),
        inverse_counts(NF, BAND),
    )
    own_source = lax.dynamic_slice_in_dim(source_order, parity, 1, 0)
    here = whiten(samples, 1, window_starts, own_source, live_mask, tables)
    devices = lax.axis_size("ch")
    there = lax.ppermute(here, "ch", [(i, i ^ 1) for i in range(devices)])
    own = whiten(samples, 0, window_starts, position[None], live_mask, tables)
    return correlate(parity[None], here, there, own, inverse_rows())


def solution(mesh):
    in_specs = (P("ch", "seg"), P("seg"), P("seg"), P("seg"))
    out_specs = P(None, None, ("seg", "ch"), None)
    return jax.shard_map(local, mesh=mesh, in_specs=in_specs, out_specs=out_specs, check_vma=False)
```

```python
import functools
import math

import jax
import jax.numpy as jnp
from jax import lax
from jax.experimental import pallas as pl
from jax.experimental.pallas import tpu as pltpu
from jax.sharding import PartitionSpec as P

CH_DEV = 128
WIN = 512
NF = 128
F0 = 4
LAGS = 128
HALF = 64
BAND = 64

STABILIZER_FLOOR = 1e-06
TILE = 128
SPAN = TILE + 2 * HALF
SRC_STEP = 32
BIN_STEP = 32
PITCH = NF + 1


def forward_rows():
    phases = (F0 + jnp.arange(NF))[:, None] * jnp.arange(WIN)[None, :] % WIN
    angles = phases.astype(jnp.float32) * (2.0 * math.pi / WIN)
    return jnp.concatenate([jnp.cos(angles), -jnp.sin(angles)], axis=0).astype(jnp.bfloat16)


def inverse_rows(scale):
    phases = (jnp.arange(LAGS)[:, None] - LAGS // 2) * (F0 + jnp.arange(NF))[None, :] % WIN
    angles = phases.astype(jnp.float32) * (2.0 * math.pi / WIN)
    rows = jnp.concatenate([jnp.cos(angles), -jnp.sin(angles)], axis=1).astype(jnp.bfloat16)
    return rows * jnp.bfloat16(scale)


def time_band():
    ahead = jnp.arange(SPAN)[None, :] - jnp.arange(TILE)[:, None]
    return ((ahead >= 0) & (ahead <= 2 * HALF)).astype(jnp.bfloat16)


def bin_band():
    apart = jnp.abs(jnp.arange(NF)[:, None] - jnp.arange(NF)[None, :])
    band = (apart <= BAND).astype(jnp.bfloat16)
    return jnp.concatenate([band, band], axis=1)


def inverse_counts(length, radius):
    at = jnp.arange(length)
    counts = jnp.minimum(at + radius + 1, length) - jnp.maximum(at - radius, 0)
    return jnp.broadcast_to((1.0 / counts.astype(jnp.float32))[:, None], (length, CH_DEV))


def pack_kernel(order_ref, x_ref, out_ref):
    blocks = out_ref.shape[0]
    numbers = order_ref.shape[0]
    for block in range(blocks):
        out_ref[block, :, :CH_DEV] = x_ref[:, block * CH_DEV : (block + 1) * CH_DEV]
        first = pl.multiple_of(order_ref[block % numbers] * CH_DEV, CH_DEV)
        out_ref[block, :, CH_DEV:] = x_ref[:, pl.ds(first, CH_DEV)]


def pack(order, recording):
    rows, channels = recording.shape
    blocks = channels // CH_DEV
    return pl.pallas_call(
        pack_kernel,
        out_shape=jax.ShapeDtypeStruct((blocks, rows, 2 * CH_DEV), recording.dtype),
        in_specs=[pl.BlockSpec(memory_space=pltpu.SMEM), pl.BlockSpec(memory_space=pltpu.VMEM)],
        out_specs=pl.BlockSpec(memory_space=pltpu.VMEM),
        name="pack",
    )(order, recording)


def whiten_kernel(
    column, rounded, starts_ref, block_ref, x_ref, first_ref, mask_ref, forward_ref, band_ref, bins_ref, tcount_ref, fcount_ref,
    out_ref, xf, means, cen, mag, nrm, total, spc, *scratch,
):
    spec = scratch[0] if rounded else out_ref
    length = x_ref.shape[0]
    windows = starts_ref.shape[0]
    pairs = windows // 2
    pitch = 2 * windows + 1
    first = pl.multiple_of(block_ref[0] * CH_DEV, CH_DEV)
    mask = mask_ref[:, pl.ds(first, CH_DEV)]
    samples = x_ref[:, column * CH_DEV : (column + 1) * CH_DEV].astype(jnp.float32) * mask
    xf[...] = samples
    at = lax.broadcasted_iota(jnp.int32, (windows, length), 1) - first_ref[...]
    inside = ((at >= 0) & (at < WIN)).astype(jnp.bfloat16)
    means[...] = jnp.dot(inside, samples.astype(jnp.bfloat16), preferred_element_type=jnp.float32) * (1.0 / WIN)
    edge = jnp.zeros((HALF, CH_DEV), jnp.bfloat16)
    for slot in range(2):
        for side in range(2):
            mag[slot][side][:HALF, :] = edge
            mag[slot][side][HALF + WIN :, :] = edge
    interior = 1.0 / (2 * HALF + 1)

    def center(pair, slot):
        for side in range(2):
            window = 2 * pair + side
            centred = xf[pl.ds(starts_ref[window], WIN), :] - means[pl.ds(window, 1), :]
            cen[slot][side][...] = centred
            mag[slot][side][HALF : HALF + WIN, :] = jnp.abs(centred).astype(jnp.bfloat16)

    def band(slot):
        for tile in range(WIN // TILE):
            rows = slice(tile * TILE, tile * TILE + SPAN)
            total[slot][tile * TILE : (tile + 1) * TILE, :] = jnp.dot(
                band_ref[...],
                jnp.concatenate([mag[slot][0][rows, :], mag[slot][1][rows, :]], axis=1),
                preferred_element_type=jnp.float32,
            )

    def normalize(pair, slot):
        for tile in range(WIN // TILE):
            rows = slice(tile * TILE, (tile + 1) * TILE)
            for side in range(2):
                running = total[slot][rows, side * CH_DEV : (side + 1) * CH_DEV]
                if HALF <= tile * TILE and (tile + 1) * TILE <= WIN - HALF:
                    running = running * interior
                else:
                    running = running * tcount_ref[rows, :]
                nrm[slot][side][rows, :] = (cen[slot][side][rows, :] / (running + STABILIZER_FLOOR)).astype(
                    jnp.bfloat16
                )

    def transform(slot):
        spc[slot][...] = jnp.dot(
            forward_ref[...],
            jnp.concatenate([nrm[slot][0][...], nrm[slot][1][...]], axis=1),
            preferred_element_type=jnp.float32,
        )

    def spectral(pair, slot):
        re, im = spc[slot][:NF, :], spc[slot][NF:, :]
        power = re * re + im * im
        amplitude = power * lax.rsqrt(jnp.maximum(power, 1e-37))
        high = amplitude.astype(jnp.bfloat16)
        low = (amplitude - high.astype(jnp.float32)).astype(jnp.bfloat16)
        sums = jnp.dot(
            bins_ref[...], jnp.concatenate([high, low], axis=0), preferred_element_type=jnp.float32
        )
        count = fcount_ref[...]
        smooth = sums * jnp.concatenate([count, count], axis=1)
        scale = 1.0 / (smooth + STABILIZER_FLOOR)
        for part in range(2):
            values = spc[slot][part * NF : (part + 1) * NF, :] * scale
            for side in range(2):
                row = part * windows + 2 * pair + side
                spec[pl.ds(row, NF, stride=pitch), :] = values[:, side * CH_DEV : (side + 1) * CH_DEV]

    for number in range(pairs + 2):
        now, before = number % 2, (number + 1) % 2
        if 1 <= number <= pairs:
            normalize(number - 1, before)
            transform(before)
        if number < pairs:
            center(number, now)
            band(now)
        if number >= 2:
            spectral(number - 2, now)

    if rounded:

        def emit(f, carry):
            out_ref[f] = spec[pl.ds(f * pitch, 2 * windows), :].astype(jnp.bfloat16)
            return carry

        lax.fori_loop(0, NF, emit, 0, unroll=8)


def whiten(samples, column, rounded, starts, block, mask, tables):
    length = samples.shape[0]
    windows = starts.shape[0]
    smem = pl.BlockSpec(memory_space=pltpu.SMEM)
    vmem = pl.BlockSpec(memory_space=pltpu.VMEM)
    padded = pltpu.VMEM((NF * (2 * windows + 1), CH_DEV), jnp.float32)
    return pl.pallas_call(
        functools.partial(whiten_kernel, column, rounded),
        out_shape=pltpu.VMEM((NF, 2 * windows, CH_DEV), jnp.bfloat16) if rounded else padded,
        in_specs=[smem, smem] + [vmem] * (3 + len(tables)),
        out_specs=vmem,
        scratch_shapes=[
            pltpu.VMEM((length, CH_DEV), jnp.float32),
            pltpu.VMEM((windows, CH_DEV), jnp.float32),
            [[pltpu.VMEM((WIN, CH_DEV), jnp.float32)] * 2] * 2,
            [[pltpu.VMEM((WIN + 2 * HALF, CH_DEV), jnp.bfloat16)] * 2] * 2,
            [[pltpu.VMEM((WIN, CH_DEV), jnp.bfloat16)] * 2] * 2,
            [pltpu.VMEM((WIN, 2 * CH_DEV), jnp.float32)] * 2,
            [pltpu.VMEM((2 * NF, 2 * CH_DEV), jnp.float32)] * 2,
        ]
        + [padded] * rounded,
        cost_estimate=pl.CostEstimate(flops=6_000_000_000, bytes_accessed=3_000_000, transcendentals=0),
        name="whiten",
        compiler_params=pltpu.CompilerParams(vmem_limit_bytes=14 * 1024 * 1024),
    )(starts, block, samples, starts.reshape(windows, 1), mask, *tables)


def correlate_kernel(parity_ref, here_ref, there_ref, own_ref, inverse_ref, out_ref, cross_re, cross_im, lag):
    bins, rows = BIN_STEP, here_ref.shape[1]
    half = rows // 2
    step = pl.program_id(0)
    crossing = NF // bins

    @pl.when(step < crossing)
    def _():
        for f in range(bins):
            at = step * bins + f
            source = jnp.concatenate([here_ref[at], there_ref[at]], axis=1)
            own = own_ref[pl.ds(at * (rows + 1), rows), :].astype(jnp.bfloat16)
            swapped = jnp.concatenate([own[half:], -own[:half]], axis=0)
            product = lax.dot_general(
                source,
                jnp.concatenate([own, swapped], axis=1),
                (((0,), (0,)), ((), ())),
                preferred_element_type=jnp.float32,
            )
            at = pl.ds(step * bins + f, 2 * CH_DEV, stride=PITCH)
            cross_re[at, :] = product[:, :CH_DEV]
            cross_im[at, :] = product[:, CH_DEV:]

    @pl.when(step >= crossing)
    def _():
        for s in range(SRC_STEP):
            out_ref[0, s] = lag[s].T
        chunk = jnp.minimum(step - crossing, 2 * CH_DEV // SRC_STEP - 1)
        base = chunk * SRC_STEP * PITCH
        for s in range(0, SRC_STEP, 2):
            columns = []
            for one in (s, s + 1):
                at = pl.ds(base + one * PITCH, NF)
                columns.append(
                    jnp.concatenate(
                        [cross_re[at, :].astype(jnp.bfloat16), cross_im[at, :].astype(jnp.bfloat16)], axis=0
                    )
                )
            lagged = jnp.dot(
                inverse_ref[...], jnp.concatenate(columns, axis=1), preferred_element_type=jnp.float32
            )
            lagged = lagged.astype(jnp.bfloat16)
            for side in range(2):
                lag[s + side] = lagged[:, side * CH_DEV : (side + 1) * CH_DEV]


def correlate(parity, here, there, own, inverse):
    crossing = NF // BIN_STEP
    chunks = CH_DEV // SRC_STEP
    spectrum = pl.BlockSpec(memory_space=pltpu.VMEM)

    def placed(i, p):
        chunk = jnp.clip(i - crossing - 1, 0, 2 * chunks - 1)
        return (chunk // chunks + p[0]) % 2, chunk % chunks, 0, 0

    return pl.pallas_call(
        correlate_kernel,
        grid_spec=pltpu.PrefetchScalarGridSpec(
            num_scalar_prefetch=1,
            grid=(crossing + 2 * chunks + 1,),
            in_specs=[spectrum, spectrum, spectrum, pl.BlockSpec(inverse.shape, lambda i, p: (0, 0))],
            out_specs=pl.BlockSpec((1, SRC_STEP, CH_DEV, LAGS), placed),
            scratch_shapes=[pltpu.VMEM((2 * CH_DEV * PITCH, CH_DEV), jnp.float32)] * 2
            + [pltpu.VMEM((SRC_STEP, LAGS, CH_DEV), jnp.bfloat16)],
        ),
        out_shape=jax.ShapeDtypeStruct((2, CH_DEV, CH_DEV, LAGS), jnp.bfloat16),
        name="correlate",
        compiler_params=pltpu.CompilerParams(vmem_limit_bytes=40 * 1024 * 1024),
    )(parity, here, there, own, inverse)


def local(recording, live_mask, window_starts, source_order):
    windows = window_starts.shape[0]
    position = lax.axis_index("ch").astype(jnp.int32)
    parity = position % 2
    sent = pack(source_order, recording)
    arrived = lax.all_to_all(sent, "ch", split_axis=0, concat_axis=0, tiled=True)
    samples = arrived.reshape(-1, 2 * CH_DEV)
    starts, mask, inverse, *tables = lax.optimization_barrier(
        (
            jnp.clip(window_starts, 0, samples.shape[0] - WIN),
            live_mask.astype(jnp.float32)[None, :],
            inverse_rows(math.sqrt(windows / NF) / windows),
            forward_rows(),
            time_band(),
            bin_band(),
            inverse_counts(WIN, HALF),
            inverse_counts(NF, BAND),
        )
    )
    own_source = lax.dynamic_slice_in_dim(source_order, parity, 1, 0)
    here = whiten(samples, 1, True, starts, own_source, mask, tables)
    devices = lax.axis_size("ch")
    there = lax.ppermute(here, "ch", [(i, i ^ 1) for i in range(devices)])
    own = whiten(samples, 0, False, starts, position[None], mask, tables)
    return correlate(parity[None], here, there, own, inverse)


def solution(mesh):
    in_specs = (P("ch", "seg"), P("seg"), P("seg"), P("seg"))
    out_specs = P(None, None, ("seg", "ch"), None)
    return jax.shard_map(local, mesh=mesh, in_specs=in_specs, out_specs=out_specs, check_vma=False)
```

```python
import functools
import math

import jax
import jax.numpy as jnp
from jax import lax
from jax.experimental import pallas as pl
from jax.experimental.pallas import tpu as pltpu
from jax.sharding import PartitionSpec as P

CH_DEV = 128
WIN = 512
NF = 128
F0 = 4
LAGS = 128
HALF = 64
BAND = 64

STABILIZER_FLOOR = 1e-06
TILE = 128
SPAN = TILE + 2 * HALF
SRC_STEP = 128
PIECE = 16
BIN_STEP = 64
PITCH = NF + 1


def forward_rows():
    phases = (F0 + jnp.arange(NF))[:, None] * jnp.arange(WIN)[None, :] % WIN
    angles = phases.astype(jnp.float32) * (2.0 * math.pi / WIN)
    return jnp.concatenate([jnp.cos(angles), -jnp.sin(angles)], axis=0).astype(jnp.bfloat16)


def inverse_rows(scale):
    phases = (jnp.arange(LAGS)[:, None] - LAGS // 2) * (F0 + jnp.arange(NF))[None, :] % WIN
    angles = phases.astype(jnp.float32) * (2.0 * math.pi / WIN)
    rows = jnp.concatenate([jnp.cos(angles), -jnp.sin(angles)], axis=1).astype(jnp.bfloat16)
    return rows * jnp.bfloat16(scale)


def time_band():
    ahead = jnp.arange(SPAN)[None, :] - jnp.arange(TILE)[:, None]
    return ((ahead >= 0) & (ahead <= 2 * HALF)).astype(jnp.bfloat16)


def bin_band():
    apart = jnp.abs(jnp.arange(NF)[:, None] - jnp.arange(NF)[None, :])
    band = (apart <= BAND).astype(jnp.bfloat16)
    return jnp.concatenate([band, band], axis=1)


def inverse_counts(length, radius):
    at = jnp.arange(length)
    counts = jnp.minimum(at + radius + 1, length) - jnp.maximum(at - radius, 0)
    return jnp.broadcast_to((1.0 / counts.astype(jnp.float32))[:, None], (length, CH_DEV))


def pack_kernel(order_ref, x_ref, out_ref):
    blocks = out_ref.shape[0]
    numbers = order_ref.shape[0]
    for block in range(blocks):
        out_ref[block, :, :CH_DEV] = x_ref[:, block * CH_DEV : (block + 1) * CH_DEV]
        first = pl.multiple_of(order_ref[block % numbers] * CH_DEV, CH_DEV)
        out_ref[block, :, CH_DEV:] = x_ref[:, pl.ds(first, CH_DEV)]


def pack(order, recording):
    rows, channels = recording.shape
    blocks = channels // CH_DEV
    return pl.pallas_call(
        pack_kernel,
        out_shape=jax.ShapeDtypeStruct((blocks, rows, 2 * CH_DEV), recording.dtype),
        in_specs=[pl.BlockSpec(memory_space=pltpu.SMEM), pl.BlockSpec(memory_space=pltpu.VMEM)],
        out_specs=pl.BlockSpec(memory_space=pltpu.VMEM),
        name="pack",
    )(order, recording)


def whiten_kernel(
    column, rounded, starts_ref, block_ref, x_ref, first_ref, mask_ref, forward_ref, band_ref, bins_ref, tcount_ref, fcount_ref,
    out_ref, xf, means, cen, mag, nrm, total, spc, *scratch,
):
    spec = scratch[0] if rounded else out_ref
    length = x_ref.shape[0]
    windows = starts_ref.shape[0]
    pairs = windows // 2
    pitch = 2 * windows + 1
    first = pl.multiple_of(block_ref[0] * CH_DEV, CH_DEV)
    mask = mask_ref[:, pl.ds(first, CH_DEV)]
    samples = x_ref[:, column * CH_DEV : (column + 1) * CH_DEV].astype(jnp.float32) * mask
    xf[...] = samples
    at = lax.broadcasted_iota(jnp.int32, (windows, length), 1) - first_ref[...]
    inside = ((at >= 0) & (at < WIN)).astype(jnp.bfloat16)
    means[...] = jnp.dot(inside, samples.astype(jnp.bfloat16), preferred_element_type=jnp.float32) * (1.0 / WIN)
    edge = jnp.zeros((HALF, CH_DEV), jnp.bfloat16)
    for slot in range(2):
        for side in range(2):
            mag[slot][side][:HALF, :] = edge
            mag[slot][side][HALF + WIN :, :] = edge
    interior = 1.0 / (2 * HALF + 1)

    def center(pair, slot):
        for side in range(2):
            window = 2 * pair + side
            centred = xf[pl.ds(starts_ref[window], WIN), :] - means[pl.ds(window, 1), :]
            cen[slot][side][...] = centred
            mag[slot][side][HALF : HALF + WIN, :] = jnp.abs(centred).astype(jnp.bfloat16)

    def band(slot):
        for tile in range(WIN // TILE):
            rows = slice(tile * TILE, tile * TILE + SPAN)
            total[slot][tile * TILE : (tile + 1) * TILE, :] = jnp.dot(
                band_ref[...],
                jnp.concatenate([mag[slot][0][rows, :], mag[slot][1][rows, :]], axis=1),
                preferred_element_type=jnp.float32,
            )

    def normalize(pair, slot):
        for tile in range(WIN // TILE):
            rows = slice(tile * TILE, (tile + 1) * TILE)
            for side in range(2):
                running = total[slot][rows, side * CH_DEV : (side + 1) * CH_DEV]
                if HALF <= tile * TILE and (tile + 1) * TILE <= WIN - HALF:
                    running = running * interior
                else:
                    running = running * tcount_ref[rows, :]
                nrm[slot][side][rows, :] = (cen[slot][side][rows, :] / (running + STABILIZER_FLOOR)).astype(
                    jnp.bfloat16
                )

    def transform(slot):
        spc[slot][...] = jnp.dot(
            forward_ref[...],
            jnp.concatenate([nrm[slot][0][...], nrm[slot][1][...]], axis=1),
            preferred_element_type=jnp.float32,
        )

    def spectral(pair, slot):
        re, im = spc[slot][:NF, :], spc[slot][NF:, :]
        power = re * re + im * im
        amplitude = power * lax.rsqrt(jnp.maximum(power, 1e-37))
        high = amplitude.astype(jnp.bfloat16)
        low = (amplitude - high.astype(jnp.float32)).astype(jnp.bfloat16)
        sums = jnp.dot(
            bins_ref[...], jnp.concatenate([high, low], axis=0), preferred_element_type=jnp.float32
        )
        count = fcount_ref[...]
        smooth = sums * jnp.concatenate([count, count], axis=1)
        scale = 1.0 / (smooth + STABILIZER_FLOOR)
        for part in range(2):
            values = spc[slot][part * NF : (part + 1) * NF, :] * scale
            for side in range(2):
                row = part * windows + 2 * pair + side
                spec[pl.ds(row, NF, stride=pitch), :] = values[:, side * CH_DEV : (side + 1) * CH_DEV]

    for number in range(pairs + 2):
        now, before = number % 2, (number + 1) % 2
        if 1 <= number <= pairs:
            normalize(number - 1, before)
            transform(before)
        if number < pairs:
            center(number, now)
            band(now)
        if number >= 2:
            spectral(number - 2, now)

    if rounded:

        def emit(f, carry):
            out_ref[f] = spec[pl.ds(f * pitch, 2 * windows), :].astype(jnp.bfloat16)
            return carry

        lax.fori_loop(0, NF, emit, 0, unroll=8)


def whiten(samples, column, rounded, starts, block, mask, tables):
    length = samples.shape[0]
    windows = starts.shape[0]
    smem = pl.BlockSpec(memory_space=pltpu.SMEM)
    vmem = pl.BlockSpec(memory_space=pltpu.VMEM)
    padded = pltpu.VMEM((NF * (2 * windows + 1), CH_DEV), jnp.float32)
    return pl.pallas_call(
        functools.partial(whiten_kernel, column, rounded),
        out_shape=pltpu.VMEM((NF, 2 * windows, CH_DEV), jnp.bfloat16) if rounded else padded,
        in_specs=[smem, smem] + [vmem] * (3 + len(tables)),
        out_specs=vmem,
        scratch_shapes=[
            pltpu.VMEM((length, CH_DEV), jnp.float32),
            pltpu.VMEM((windows, CH_DEV), jnp.float32),
            [[pltpu.VMEM((WIN, CH_DEV), jnp.float32)] * 2] * 2,
            [[pltpu.VMEM((WIN + 2 * HALF, CH_DEV), jnp.bfloat16)] * 2] * 2,
            [[pltpu.VMEM((WIN, CH_DEV), jnp.bfloat16)] * 2] * 2,
            [pltpu.VMEM((WIN, 2 * CH_DEV), jnp.float32)] * 2,
            [pltpu.VMEM((2 * NF, 2 * CH_DEV), jnp.float32)] * 2,
        ]
        + [padded] * rounded,
        cost_estimate=pl.CostEstimate(flops=6_000_000_000, bytes_accessed=3_000_000, transcendentals=0),
        name="whiten",
        compiler_params=pltpu.CompilerParams(vmem_limit_bytes=14 * 1024 * 1024),
    )(starts, block, samples, starts.reshape(windows, 1), mask, *tables)


def correlate_kernel(
    parity_ref, here_ref, there_ref, own_ref, inverse_ref, out_ref, cross_re, cross_im, lags, sent
):
    rows = here_ref.shape[1]
    half = rows // 2

    def cross(step, carry):
        for f in range(BIN_STEP):
            at = step * BIN_STEP + f
            source = jnp.concatenate([here_ref[at], there_ref[at]], axis=1)
            own = own_ref[pl.ds(at * (rows + 1), rows), :].astype(jnp.bfloat16)
            swapped = jnp.concatenate([own[half:], -own[:half]], axis=0)
            product = lax.dot_general(
                source,
                jnp.concatenate([own, swapped], axis=1),
                (((0,), (0,)), ((), ())),
                preferred_element_type=jnp.float32,
            )
            to = pl.ds(at, 2 * CH_DEV, stride=PITCH)
            cross_re[to, :] = product[:, :CH_DEV]
            cross_im[to, :] = product[:, CH_DEV:]
        return carry

    lax.fori_loop(0, NF // BIN_STEP, cross, 0)

    def copy(first):
        block, source = (first // CH_DEV + parity_ref[0]) % 2, first % CH_DEV
        return pltpu.make_async_copy(
            lags.at[pl.ds(first, PIECE)], out_ref.at[block, pl.ds(source, PIECE)], sent.at[first // PIECE]
        )

    def lag(step, carry):
        first = step * SRC_STEP
        for s in range(0, SRC_STEP, 2):
            columns = []
            for one in (s, s + 1):
                at = pl.ds((first + one) * PITCH, NF)
                columns.append(
                    jnp.concatenate(
                        [cross_re[at, :].astype(jnp.bfloat16), cross_im[at, :].astype(jnp.bfloat16)], axis=0
                    )
                )
            lagged = jnp.dot(
                inverse_ref[...], jnp.concatenate(columns, axis=1), preferred_element_type=jnp.float32
            ).astype(jnp.bfloat16)
            for side in range(2):
                lags[first + s + side] = lagged[:, side * CH_DEV : (side + 1) * CH_DEV].T
            if (s + 2) % PIECE == 0:
                copy(first + s + 2 - PIECE).start()
        return carry

    lax.fori_loop(0, 2 * CH_DEV // SRC_STEP, lag, 0)
    for number in range(2 * CH_DEV // PIECE):
        copy(number * PIECE).wait()


def correlate(parity, here, there, own, inverse):
    vmem = pl.BlockSpec(memory_space=pltpu.VMEM)
    return pl.pallas_call(
        correlate_kernel,
        in_specs=[pl.BlockSpec(memory_space=pltpu.SMEM)] + [vmem] * 4,
        out_specs=pl.BlockSpec(memory_space=pl.ANY),
        out_shape=jax.ShapeDtypeStruct((2, CH_DEV, CH_DEV, LAGS), jnp.bfloat16),
        scratch_shapes=[pltpu.VMEM((2 * CH_DEV * PITCH, CH_DEV), jnp.float32)] * 2
        + [
            pltpu.VMEM((2 * CH_DEV, CH_DEV, LAGS), jnp.bfloat16),
            pltpu.SemaphoreType.DMA((2 * CH_DEV // PIECE,)),
        ],
        name="correlate",
        compiler_params=pltpu.CompilerParams(vmem_limit_bytes=44 * 1024 * 1024),
    )(parity, here, there, own, inverse)


def local(recording, live_mask, window_starts, source_order):
    windows = window_starts.shape[0]
    position = lax.axis_index("ch").astype(jnp.int32)
    parity = position % 2
    sent = pack(source_order, recording)
    arrived = lax.all_to_all(sent, "ch", split_axis=0, concat_axis=0, tiled=True)
    samples = arrived.reshape(-1, 2 * CH_DEV)
    starts, mask, inverse, *tables = lax.optimization_barrier(
        (
            jnp.clip(window_starts, 0, samples.shape[0] - WIN),
            live_mask.astype(jnp.float32)[None, :],
            inverse_rows(math.sqrt(windows / NF) / windows),
            forward_rows(),
            time_band(),
            bin_band(),
            inverse_counts(WIN, HALF),
            inverse_counts(NF, BAND),
        )
    )
    own_source = lax.dynamic_slice_in_dim(source_order, parity, 1, 0)
    here = whiten(samples, 1, True, starts, own_source, mask, tables)
    devices = lax.axis_size("ch")
    there = lax.ppermute(here, "ch", [(i, i ^ 1) for i in range(devices)])
    own = whiten(samples, 0, False, starts, position[None], mask, tables)
    return correlate(parity[None], here, there, own, inverse)


def solution(mesh):
    in_specs = (P("ch", "seg"), P("seg"), P("seg"), P("seg"))
    out_specs = P(None, None, ("seg", "ch"), None)
    return jax.shard_map(local, mesh=mesh, in_specs=in_specs, out_specs=out_specs, check_vma=False)
```

```python
import functools
import math

import jax
import jax.numpy as jnp
from jax import lax
from jax.experimental import pallas as pl
from jax.experimental.pallas import tpu as pltpu
from jax.sharding import PartitionSpec as P

CH_DEV = 128
WIN = 512
NF = 128
F0 = 4
LAGS = 128
HALF = 64
BAND = 64

STABILIZER_FLOOR = 1e-06
TILE = 128
SPAN = TILE + 2 * HALF
SRC_STEP = 256
PIECE = 16
BIN_STEP = 128
PITCH = NF + 1


def forward_rows():
    phases = (F0 + jnp.arange(NF))[:, None] * jnp.arange(WIN)[None, :] % WIN
    angles = phases.astype(jnp.float32) * (2.0 * math.pi / WIN)
    return jnp.concatenate([jnp.cos(angles), -jnp.sin(angles)], axis=0).astype(jnp.bfloat16)


def inverse_rows(scale):
    phases = (jnp.arange(LAGS)[:, None] - LAGS // 2) * (F0 + jnp.arange(NF))[None, :] % WIN
    angles = phases.astype(jnp.float32) * (2.0 * math.pi / WIN)
    rows = jnp.concatenate([jnp.cos(angles), -jnp.sin(angles)], axis=1).astype(jnp.bfloat16)
    return rows * jnp.bfloat16(scale)


def time_band():
    ahead = jnp.arange(SPAN)[None, :] - jnp.arange(TILE)[:, None]
    return ((ahead >= 0) & (ahead <= 2 * HALF)).astype(jnp.bfloat16)


def bin_band():
    apart = jnp.abs(jnp.arange(NF)[:, None] - jnp.arange(NF)[None, :])
    band = (apart <= BAND).astype(jnp.bfloat16)
    return jnp.concatenate([band, band], axis=1)


def inverse_counts(length, radius):
    at = jnp.arange(length)
    counts = jnp.minimum(at + radius + 1, length) - jnp.maximum(at - radius, 0)
    return jnp.broadcast_to((1.0 / counts.astype(jnp.float32))[:, None], (length, CH_DEV))


def pack_kernel(order_ref, x_ref, out_ref):
    blocks = out_ref.shape[0]
    numbers = order_ref.shape[0]
    for block in range(blocks):
        out_ref[block, :, :CH_DEV] = x_ref[:, block * CH_DEV : (block + 1) * CH_DEV]
        first = pl.multiple_of(order_ref[block % numbers] * CH_DEV, CH_DEV)
        out_ref[block, :, CH_DEV:] = x_ref[:, pl.ds(first, CH_DEV)]


def pack(order, recording):
    rows, channels = recording.shape
    blocks = channels // CH_DEV
    return pl.pallas_call(
        pack_kernel,
        out_shape=jax.ShapeDtypeStruct((blocks, rows, 2 * CH_DEV), recording.dtype),
        in_specs=[pl.BlockSpec(memory_space=pltpu.SMEM), pl.BlockSpec(memory_space=pltpu.VMEM)],
        out_specs=pl.BlockSpec(memory_space=pltpu.VMEM),
        name="pack",
    )(order, recording)


def whiten_kernel(
    column, rounded, starts_ref, block_ref, x_ref, first_ref, mask_ref, forward_ref, band_ref, bins_ref, tcount_ref, fcount_ref,
    out_ref, xf, means, cen, mag, nrm, total, spc, *scratch,
):
    spec = scratch[0] if rounded else out_ref
    length = x_ref.shape[0]
    windows = starts_ref.shape[0]
    pairs = windows // 2
    pitch = 2 * windows + 1
    first = pl.multiple_of(block_ref[0] * CH_DEV, CH_DEV)
    mask = mask_ref[:, pl.ds(first, CH_DEV)]
    samples = x_ref[:, column * CH_DEV : (column + 1) * CH_DEV].astype(jnp.float32) * mask
    xf[...] = samples
    at = lax.broadcasted_iota(jnp.int32, (windows, length), 1) - first_ref[...]
    inside = ((at >= 0) & (at < WIN)).astype(jnp.bfloat16)
    means[...] = jnp.dot(inside, samples.astype(jnp.bfloat16), preferred_element_type=jnp.float32) * (1.0 / WIN)
    edge = jnp.zeros((HALF, CH_DEV), jnp.bfloat16)
    for slot in range(2):
        for side in range(2):
            mag[slot][side][:HALF, :] = edge
            mag[slot][side][HALF + WIN :, :] = edge
    interior = 1.0 / (2 * HALF + 1)

    def center(pair, slot):
        for side in range(2):
            window = 2 * pair + side
            centred = xf[pl.ds(starts_ref[window], WIN), :] - means[pl.ds(window, 1), :]
            cen[slot][side][...] = centred
            mag[slot][side][HALF : HALF + WIN, :] = jnp.abs(centred).astype(jnp.bfloat16)

    def band(slot):
        for tile in range(WIN // TILE):
            rows = slice(tile * TILE, tile * TILE + SPAN)
            total[slot][tile * TILE : (tile + 1) * TILE, :] = jnp.dot(
                band_ref[...],
                jnp.concatenate([mag[slot][0][rows, :], mag[slot][1][rows, :]], axis=1),
                preferred_element_type=jnp.float32,
            )

    def normalize(pair, slot):
        for tile in range(WIN // TILE):
            rows = slice(tile * TILE, (tile + 1) * TILE)
            for side in range(2):
                running = total[slot][rows, side * CH_DEV : (side + 1) * CH_DEV]
                if HALF <= tile * TILE and (tile + 1) * TILE <= WIN - HALF:
                    running = running * interior
                else:
                    running = running * tcount_ref[rows, :]
                nrm[slot][side][rows, :] = (cen[slot][side][rows, :] / (running + STABILIZER_FLOOR)).astype(
                    jnp.bfloat16
                )

    def transform(slot):
        spc[slot][...] = jnp.dot(
            forward_ref[...],
            jnp.concatenate([nrm[slot][0][...], nrm[slot][1][...]], axis=1),
            preferred_element_type=jnp.float32,
        )

    def spectral(pair, slot):
        re, im = spc[slot][:NF, :], spc[slot][NF:, :]
        power = re * re + im * im
        amplitude = power * lax.rsqrt(jnp.maximum(power, 1e-37))
        high = amplitude.astype(jnp.bfloat16)
        low = (amplitude - high.astype(jnp.float32)).astype(jnp.bfloat16)
        sums = jnp.dot(
            bins_ref[...], jnp.concatenate([high, low], axis=0), preferred_element_type=jnp.float32
        )
        count = fcount_ref[...]
        smooth = sums * jnp.concatenate([count, count], axis=1)
        scale = 1.0 / (smooth + STABILIZER_FLOOR)
        for part in range(2):
            values = spc[slot][part * NF : (part + 1) * NF, :] * scale
            for side in range(2):
                row = part * windows + 2 * pair + side
                spec[pl.ds(row, NF, stride=pitch), :] = values[:, side * CH_DEV : (side + 1) * CH_DEV]

    for number in range(pairs + 2):
        now, before = number % 2, (number + 1) % 2
        if 1 <= number <= pairs:
            normalize(number - 1, before)
            transform(before)
        if number < pairs:
            center(number, now)
            band(now)
        if number >= 2:
            spectral(number - 2, now)

    if rounded:

        def emit(f, carry):
            out_ref[f] = spec[pl.ds(f * pitch, 2 * windows), :].astype(jnp.bfloat16)
            return carry

        lax.fori_loop(0, NF, emit, 0, unroll=8)


def whiten(samples, column, rounded, starts, block, mask, tables):
    length = samples.shape[0]
    windows = starts.shape[0]
    smem = pl.BlockSpec(memory_space=pltpu.SMEM)
    vmem = pl.BlockSpec(memory_space=pltpu.VMEM)
    padded = pltpu.VMEM((NF * (2 * windows + 1), CH_DEV), jnp.float32)
    return pl.pallas_call(
        functools.partial(whiten_kernel, column, rounded),
        out_shape=pltpu.VMEM((NF, 2 * windows, CH_DEV), jnp.bfloat16) if rounded else padded,
        in_specs=[smem, smem] + [vmem] * (3 + len(tables)),
        out_specs=vmem,
        scratch_shapes=[
            pltpu.VMEM((length, CH_DEV), jnp.float32),
            pltpu.VMEM((windows, CH_DEV), jnp.float32),
            [[pltpu.VMEM((WIN, CH_DEV), jnp.float32)] * 2] * 2,
            [[pltpu.VMEM((WIN + 2 * HALF, CH_DEV), jnp.bfloat16)] * 2] * 2,
            [[pltpu.VMEM((WIN, CH_DEV), jnp.bfloat16)] * 2] * 2,
            [pltpu.VMEM((WIN, 2 * CH_DEV), jnp.float32)] * 2,
            [pltpu.VMEM((2 * NF, 2 * CH_DEV), jnp.float32)] * 2,
        ]
        + [padded] * rounded,
        cost_estimate=pl.CostEstimate(flops=6_000_000_000, bytes_accessed=3_000_000, transcendentals=0),
        name="whiten",
        compiler_params=pltpu.CompilerParams(vmem_limit_bytes=14 * 1024 * 1024),
    )(starts, block, samples, starts.reshape(windows, 1), mask, *tables)


def correlate_kernel(
    parity_ref, here_ref, there_ref, own_ref, inverse_ref, out_ref, cross_re, cross_im, lags, sent
):
    rows = here_ref.shape[1]
    half = rows // 2

    def cross(step, carry):
        for f in range(BIN_STEP):
            at = step * BIN_STEP + f
            source = jnp.concatenate([here_ref[at], there_ref[at]], axis=1)
            own = own_ref[pl.ds(at * (rows + 1), rows), :].astype(jnp.bfloat16)
            swapped = jnp.concatenate([own[half:], -own[:half]], axis=0)
            product = lax.dot_general(
                source,
                jnp.concatenate([own, swapped], axis=1),
                (((0,), (0,)), ((), ())),
                preferred_element_type=jnp.float32,
            )
            to = pl.ds(at, 2 * CH_DEV, stride=PITCH)
            cross_re[to, :] = product[:, :CH_DEV]
            cross_im[to, :] = product[:, CH_DEV:]
        return carry

    lax.fori_loop(0, NF // BIN_STEP, cross, 0)

    def copy(first):
        block, source = (first // CH_DEV + parity_ref[0]) % 2, first % CH_DEV
        return pltpu.make_async_copy(
            lags.at[pl.ds(first, PIECE)], out_ref.at[block, pl.ds(source, PIECE)], sent.at[first // PIECE]
        )

    def lag(step, carry):
        first = step * SRC_STEP
        for s in range(0, SRC_STEP, 2):
            columns = []
            for one in (s, s + 1):
                at = pl.ds((first + one) * PITCH, NF)
                columns.append(
                    jnp.concatenate(
                        [cross_re[at, :].astype(jnp.bfloat16), cross_im[at, :].astype(jnp.bfloat16)], axis=0
                    )
                )
            lagged = jnp.dot(
                inverse_ref[...], jnp.concatenate(columns, axis=1), preferred_element_type=jnp.float32
            ).astype(jnp.bfloat16)
            for side in range(2):
                lags[first + s + side] = lagged[:, side * CH_DEV : (side + 1) * CH_DEV].T
            if (s + 2) % PIECE == 0:
                copy(first + s + 2 - PIECE).start()
        return carry

    lax.fori_loop(0, 2 * CH_DEV // SRC_STEP, lag, 0)
    for number in range(2 * CH_DEV // PIECE):
        copy(number * PIECE).wait()


def correlate(parity, here, there, own, inverse):
    vmem = pl.BlockSpec(memory_space=pltpu.VMEM)
    return pl.pallas_call(
        correlate_kernel,
        in_specs=[pl.BlockSpec(memory_space=pltpu.SMEM)] + [vmem] * 4,
        out_specs=pl.BlockSpec(memory_space=pl.ANY),
        out_shape=jax.ShapeDtypeStruct((2, CH_DEV, CH_DEV, LAGS), jnp.bfloat16),
        scratch_shapes=[pltpu.VMEM((2 * CH_DEV * PITCH, CH_DEV), jnp.float32)] * 2
        + [
            pltpu.VMEM((2 * CH_DEV, CH_DEV, LAGS), jnp.bfloat16),
            pltpu.SemaphoreType.DMA((2 * CH_DEV // PIECE,)),
        ],
        name="correlate",
        compiler_params=pltpu.CompilerParams(vmem_limit_bytes=44 * 1024 * 1024),
    )(parity, here, there, own, inverse)


def local(recording, live_mask, window_starts, source_order):
    windows = window_starts.shape[0]
    position = lax.axis_index("ch").astype(jnp.int32)
    parity = position % 2
    sent = pack(source_order, recording)
    arrived = lax.all_to_all(sent, "ch", split_axis=0, concat_axis=0, tiled=True)
    samples = arrived.reshape(-1, 2 * CH_DEV)
    starts, mask, inverse, *tables = lax.optimization_barrier(
        (
            jnp.clip(window_starts, 0, samples.shape[0] - WIN),
            live_mask.astype(jnp.float32)[None, :],
            inverse_rows(math.sqrt(windows / NF) / windows),
            forward_rows(),
            time_band(),
            bin_band(),
            inverse_counts(WIN, HALF),
            inverse_counts(NF, BAND),
        )
    )
    own_source = lax.dynamic_slice_in_dim(source_order, parity, 1, 0)
    here = whiten(samples, 1, True, starts, own_source, mask, tables)
    devices = lax.axis_size("ch")
    there = lax.ppermute(here, "ch", [(i, i ^ 1) for i in range(devices)])
    own = whiten(samples, 0, False, starts, position[None], mask, tables)
    return correlate(parity[None], here, there, own, inverse)


def solution(mesh):
    in_specs = (P("ch", "seg"), P("seg"), P("seg"), P("seg"))
    out_specs = P(None, None, ("seg", "ch"), None)
    return jax.shard_map(local, mesh=mesh, in_specs=in_specs, out_specs=out_specs, check_vma=False)
```

```python
import functools
import math

import jax
import jax.numpy as jnp
from jax import lax
from jax.experimental import pallas as pl
from jax.experimental.pallas import tpu as pltpu
from jax.sharding import PartitionSpec as P

CH_DEV = 128
WIN = 512
NF = 128
F0 = 4
LAGS = 128
HALF = 64
BAND = 64

STABILIZER_FLOOR = 1e-06
TILE = 128
SPAN = TILE + 2 * HALF
SRC_STEP = 256
PIECE = 8
BIN_STEP = 128
PITCH = NF + 1


def forward_rows():
    phases = (F0 + jnp.arange(NF))[:, None] * jnp.arange(WIN)[None, :] % WIN
    angles = phases.astype(jnp.float32) * (2.0 * math.pi / WIN)
    return jnp.concatenate([jnp.cos(angles), -jnp.sin(angles)], axis=0).astype(jnp.bfloat16)


def inverse_rows(scale):
    phases = (jnp.arange(LAGS)[:, None] - LAGS // 2) * (F0 + jnp.arange(NF))[None, :] % WIN
    angles = phases.astype(jnp.float32) * (2.0 * math.pi / WIN)
    rows = jnp.concatenate([jnp.cos(angles), -jnp.sin(angles)], axis=1).astype(jnp.bfloat16)
    return rows * jnp.bfloat16(scale)


def time_band():
    ahead = jnp.arange(SPAN)[None, :] - jnp.arange(TILE)[:, None]
    return ((ahead >= 0) & (ahead <= 2 * HALF)).astype(jnp.bfloat16)


def bin_band():
    apart = jnp.abs(jnp.arange(NF)[:, None] - jnp.arange(NF)[None, :])
    band = (apart <= BAND).astype(jnp.bfloat16)
    return jnp.concatenate([band, band], axis=1)


def inverse_counts(length, radius):
    at = jnp.arange(length)
    counts = jnp.minimum(at + radius + 1, length) - jnp.maximum(at - radius, 0)
    return jnp.broadcast_to((1.0 / counts.astype(jnp.float32))[:, None], (length, CH_DEV))


def pack_kernel(order_ref, x_ref, out_ref):
    blocks = out_ref.shape[0]
    numbers = order_ref.shape[0]
    for block in range(blocks):
        out_ref[block, :, :CH_DEV] = x_ref[:, block * CH_DEV : (block + 1) * CH_DEV]
        first = pl.multiple_of(order_ref[block % numbers] * CH_DEV, CH_DEV)
        out_ref[block, :, CH_DEV:] = x_ref[:, pl.ds(first, CH_DEV)]


def pack(order, recording):
    rows, channels = recording.shape
    blocks = channels // CH_DEV
    return pl.pallas_call(
        pack_kernel,
        out_shape=jax.ShapeDtypeStruct((blocks, rows, 2 * CH_DEV), recording.dtype),
        in_specs=[pl.BlockSpec(memory_space=pltpu.SMEM), pl.BlockSpec(memory_space=pltpu.VMEM)],
        out_specs=pl.BlockSpec(memory_space=pltpu.VMEM),
        name="pack",
    )(order, recording)


def whiten_kernel(
    column, rounded, starts_ref, block_ref, x_ref, first_ref, mask_ref, forward_ref, band_ref, bins_ref, tcount_ref, fcount_ref,
    out_ref, xf, means, cen, mag, nrm, total, spc, *scratch,
):
    spec = scratch[0] if rounded else out_ref
    length = x_ref.shape[0]
    windows = starts_ref.shape[0]
    pairs = windows // 2
    pitch = 2 * windows + 1
    first = pl.multiple_of(block_ref[0] * CH_DEV, CH_DEV)
    mask = mask_ref[:, pl.ds(first, CH_DEV)]
    samples = x_ref[:, column * CH_DEV : (column + 1) * CH_DEV].astype(jnp.float32) * mask
    xf[...] = samples
    at = lax.broadcasted_iota(jnp.int32, (windows, length), 1) - first_ref[...]
    inside = ((at >= 0) & (at < WIN)).astype(jnp.bfloat16)
    means[...] = jnp.dot(inside, samples.astype(jnp.bfloat16), preferred_element_type=jnp.float32) * (1.0 / WIN)
    edge = jnp.zeros((HALF, CH_DEV), jnp.bfloat16)
    for slot in range(2):
        for side in range(2):
            mag[slot][side][:HALF, :] = edge
            mag[slot][side][HALF + WIN :, :] = edge
    interior = 1.0 / (2 * HALF + 1)

    def center(pair, slot):
        for side in range(2):
            window = 2 * pair + side
            centred = xf[pl.ds(starts_ref[window], WIN), :] - means[pl.ds(window, 1), :]
            cen[slot][side][...] = centred
            mag[slot][side][HALF : HALF + WIN, :] = jnp.abs(centred).astype(jnp.bfloat16)

    def band(slot):
        for tile in range(WIN // TILE):
            rows = slice(tile * TILE, tile * TILE + SPAN)
            total[slot][tile * TILE : (tile + 1) * TILE, :] = jnp.dot(
                band_ref[...],
                jnp.concatenate([mag[slot][0][rows, :], mag[slot][1][rows, :]], axis=1),
                preferred_element_type=jnp.float32,
            )

    def normalize(pair, slot):
        for tile in range(WIN // TILE):
            rows = slice(tile * TILE, (tile + 1) * TILE)
            for side in range(2):
                running = total[slot][rows, side * CH_DEV : (side + 1) * CH_DEV]
                if HALF <= tile * TILE and (tile + 1) * TILE <= WIN - HALF:
                    running = running * interior
                else:
                    running = running * tcount_ref[rows, :]
                nrm[slot][side][rows, :] = (cen[slot][side][rows, :] / (running + STABILIZER_FLOOR)).astype(
                    jnp.bfloat16
                )

    def transform(slot):
        spc[slot][...] = jnp.dot(
            forward_ref[...],
            jnp.concatenate([nrm[slot][0][...], nrm[slot][1][...]], axis=1),
            preferred_element_type=jnp.float32,
        )

    def spectral(pair, slot):
        re, im = spc[slot][:NF, :], spc[slot][NF:, :]
        power = re * re + im * im
        amplitude = power * lax.rsqrt(jnp.maximum(power, 1e-37))
        high = amplitude.astype(jnp.bfloat16)
        low = (amplitude - high.astype(jnp.float32)).astype(jnp.bfloat16)
        sums = jnp.dot(
            bins_ref[...], jnp.concatenate([high, low], axis=0), preferred_element_type=jnp.float32
        )
        count = fcount_ref[...]
        smooth = sums * jnp.concatenate([count, count], axis=1)
        scale = 1.0 / (smooth + STABILIZER_FLOOR)
        for part in range(2):
            values = spc[slot][part * NF : (part + 1) * NF, :] * scale
            for side in range(2):
                row = part * windows + 2 * pair + side
                spec[pl.ds(row, NF, stride=pitch), :] = values[:, side * CH_DEV : (side + 1) * CH_DEV]

    for number in range(pairs + 2):
        now, before = number % 2, (number + 1) % 2
        if 1 <= number <= pairs:
            normalize(number - 1, before)
            transform(before)
        if number < pairs:
            center(number, now)
            band(now)
        if number >= 2:
            spectral(number - 2, now)

    if rounded:

        def emit(f, carry):
            out_ref[f] = spec[pl.ds(f * pitch, 2 * windows), :].astype(jnp.bfloat16)
            return carry

        lax.fori_loop(0, NF, emit, 0, unroll=8)


def whiten(samples, column, rounded, starts, block, mask, tables):
    length = samples.shape[0]
    windows = starts.shape[0]
    smem = pl.BlockSpec(memory_space=pltpu.SMEM)
    vmem = pl.BlockSpec(memory_space=pltpu.VMEM)
    padded = pltpu.VMEM((NF * (2 * windows + 1), CH_DEV), jnp.float32)
    return pl.pallas_call(
        functools.partial(whiten_kernel, column, rounded),
        out_shape=pltpu.VMEM((NF, 2 * windows, CH_DEV), jnp.bfloat16) if rounded else padded,
        in_specs=[smem, smem] + [vmem] * (3 + len(tables)),
        out_specs=vmem,
        scratch_shapes=[
            pltpu.VMEM((length, CH_DEV), jnp.float32),
            pltpu.VMEM((windows, CH_DEV), jnp.float32),
            [[pltpu.VMEM((WIN, CH_DEV), jnp.float32)] * 2] * 2,
            [[pltpu.VMEM((WIN + 2 * HALF, CH_DEV), jnp.bfloat16)] * 2] * 2,
            [[pltpu.VMEM((WIN, CH_DEV), jnp.bfloat16)] * 2] * 2,
            [pltpu.VMEM((WIN, 2 * CH_DEV), jnp.float32)] * 2,
            [pltpu.VMEM((2 * NF, 2 * CH_DEV), jnp.float32)] * 2,
        ]
        + [padded] * rounded,
        cost_estimate=pl.CostEstimate(flops=6_000_000_000, bytes_accessed=3_000_000, transcendentals=0),
        name="whiten",
        compiler_params=pltpu.CompilerParams(
            vmem_limit_bytes=14 * 1024 * 1024
        ),
    )(starts, block, samples, starts.reshape(windows, 1), mask, *tables)


def correlate_kernel(
    parity_ref, here_ref, there_ref, own_ref, inverse_ref, out_ref, cross_re, cross_im, lags, sent
):
    rows = here_ref.shape[1]
    half = rows // 2

    def cross(step, carry):
        for f in range(BIN_STEP):
            at = step * BIN_STEP + f
            source = jnp.concatenate([here_ref[at], there_ref[at]], axis=1)
            own = own_ref[pl.ds(at * (rows + 1), rows), :].astype(jnp.bfloat16)
            swapped = jnp.concatenate([own[half:], -own[:half]], axis=0)
            product = lax.dot_general(
                source,
                jnp.concatenate([own, swapped], axis=1),
                (((0,), (0,)), ((), ())),
                preferred_element_type=jnp.float32,
            )
            to = pl.ds(at, 2 * CH_DEV, stride=PITCH)
            cross_re[to, :] = product[:, :CH_DEV]
            cross_im[to, :] = product[:, CH_DEV:]
        return carry

    lax.fori_loop(0, NF // BIN_STEP, cross, 0)

    def copy(first):
        block, source = (first // CH_DEV + parity_ref[0]) % 2, first % CH_DEV
        return pltpu.make_async_copy(
            lags.at[pl.ds(first, PIECE)], out_ref.at[block, pl.ds(source, PIECE)], sent.at[first // PIECE]
        )

    def lag(step, carry):
        first = step * SRC_STEP
        for s in range(0, SRC_STEP, 2):
            columns = []
            for one in (s, s + 1):
                at = pl.ds((first + one) * PITCH, NF)
                columns.append(
                    jnp.concatenate(
                        [cross_re[at, :].astype(jnp.bfloat16), cross_im[at, :].astype(jnp.bfloat16)], axis=0
                    )
                )
            lagged = jnp.dot(
                inverse_ref[...], jnp.concatenate(columns, axis=1), preferred_element_type=jnp.float32
            ).astype(jnp.bfloat16)
            for side in range(2):
                lags[first + s + side] = lagged[:, side * CH_DEV : (side + 1) * CH_DEV].T
            if (s + 2) % PIECE == 0:
                copy(first + s + 2 - PIECE).start()
        return carry

    lax.fori_loop(0, 2 * CH_DEV // SRC_STEP, lag, 0)
    for number in range(2 * CH_DEV // PIECE):
        copy(number * PIECE).wait()


def correlate(parity, here, there, own, inverse):
    vmem = pl.BlockSpec(memory_space=pltpu.VMEM)
    return pl.pallas_call(
        correlate_kernel,
        in_specs=[pl.BlockSpec(memory_space=pltpu.SMEM)] + [vmem] * 4,
        out_specs=pl.BlockSpec(memory_space=pl.ANY),
        out_shape=jax.ShapeDtypeStruct((2, CH_DEV, CH_DEV, LAGS), jnp.bfloat16),
        scratch_shapes=[pltpu.VMEM((2 * CH_DEV * PITCH, CH_DEV), jnp.float32)] * 2
        + [
            pltpu.VMEM((2 * CH_DEV, CH_DEV, LAGS), jnp.bfloat16),
            pltpu.SemaphoreType.DMA((2 * CH_DEV // PIECE,)),
        ],
        name="correlate",
        compiler_params=pltpu.CompilerParams(vmem_limit_bytes=44 * 1024 * 1024),
    )(parity, here, there, own, inverse)


def local(recording, live_mask, window_starts, source_order):
    windows = window_starts.shape[0]
    position = lax.axis_index("ch").astype(jnp.int32)
    parity = position % 2
    sent = pack(source_order, recording)
    arrived = lax.all_to_all(sent, "ch", split_axis=0, concat_axis=0, tiled=True)
    samples = arrived.reshape(-1, 2 * CH_DEV)
    starts, mask, inverse, *tables = lax.optimization_barrier(
        (
            jnp.clip(window_starts, 0, samples.shape[0] - WIN),
            live_mask.astype(jnp.float32)[None, :],
            inverse_rows(math.sqrt(windows / NF) / windows),
            forward_rows(),
            time_band(),
            bin_band(),
            inverse_counts(WIN, HALF),
            inverse_counts(NF, BAND),
        )
    )
    own_source = lax.dynamic_slice_in_dim(source_order, parity, 1, 0)
    here = whiten(samples, 1, True, starts, own_source, mask, tables)
    devices = lax.axis_size("ch")
    there = lax.ppermute(here, "ch", [(i, i ^ 1) for i in range(devices)])
    own = whiten(samples, 0, False, starts, position[None], mask, tables)
    return correlate(parity[None], here, there, own, inverse)


def solution(mesh):
    in_specs = (P("ch", "seg"), P("seg"), P("seg"), P("seg"))
    out_specs = P(None, None, ("seg", "ch"), None)
    return jax.shard_map(local, mesh=mesh, in_specs=in_specs, out_specs=out_specs, check_vma=False)
```
